512 devices in a mesh: dp: 16 (over z, core), head: 8 (over y), tok: 4 (over x).
Axes of the slice: x: 4, y: 8, z: 8, core: 2. Of those that a mesh axis runs over, the one named last changes fastest.
Arguments:
- mamba_input: bfloat16 [32, 64, 8192], P('dp', 'tok', 'head'), may hold values from -6 to 6
- gate_input: bfloat16 [32, 64, 8192], P('dp', 'tok', 'head'), may hold values from -6 to 6
- in_b: bfloat16 [32, 64, 1024], P('dp', 'tok', 'head'), may hold values from -0.75 to 0.75
- in_c: bfloat16 [32, 64, 1024], P('dp', 'tok', 'head'), may hold values from -0.75 to 0.75
- step_size: bfloat16 [32, 64, 128], P('dp', 'tok', 'head'), may hold values from 0.019897461 to 1
- decay_rate: float32 [128], P('head'), may hold values from 0.01 to 1
- skip_weight: float32 [128], P('head'), may hold values from 0.5 to 1.5
- norm_gain: float32 [8192], P('head'), may hold values from 0.1 to 1.9
- ssm_state: bfloat16 [32, 128, 64, 128], P('dp', 'head', None, 'tok'), may hold values from -6 to 6
- out_weight: bfloat16 [8192, 4096], P(('head', 'tok')), may hold values from -0.0625 to 0.0625
- queries: bfloat16 [32, 64, 4096], P('dp', 'tok', 'head'), may hold values from -6 to 6
- draft_token_keys: bfloat16 [32, 64, 1024], P('dp', 'tok', 'head'), may hold values from -6 to 6
- draft_values: bfloat16 [32, 64, 1024], P('dp', 'tok', 'head'), may hold values from -6 to 6
- cached_key_rows: bfloat16 [32, 4096, 1024], P('dp', 'tok', 'head'), may hold values from -4 to 4
- cache_values: bfloat16 [32, 4096, 1024], P('dp', 'tok', 'head'), may hold values from -6 to 6
- cache_len: int32 [32], P('dp'), may hold values from 2 to 4096
- accepted: int32 [32], P('dp'), may hold values from 0 to 64
Outputs:
- mamba_out: bfloat16 [64, 32, 4096], P(('head', 'tok'), 'dp')
- attn_context: bfloat16 [32, 64, 4096], P('dp', 'tok', 'head')
- committed_state: bfloat16 [32, 128, 64, 128], P('dp', 'head', None, 'tok')
The draws below stay inside these ranges and needn't reach their ends.
Inputs may be any that keep to these rules, and one draw needn't show every extreme that they name: Each sequence's cached positions 0 to cache_len - 1 are valid.
All inputs are finite; a program needn't handle non-finite values.
Results may differ from the reference program's by a relative error of at most 0.018.
Values may be sent and summed in bfloat16 or wider, within the bound.
No kernel may reach another device: no remote copies, remote signals or barrier semaphores. Data moves between devices by JAX's collectives and lax.ppermute only.
A program may use at most 64 MiB of HBM per device.

```python
import math
import jax
import jax.numpy as jnp
from jax import lax

D = 4096
STATE = 128
HEAD_DIM = 64
ATT_DIM = 128
HEADS = 128
GROUPS = 8
QHEADS = 32
KVHEADS = 8
DRAFT = 64
CACHE = 4096
BATCH = 32
N_HEAD = 8
N_TOK = 4


def draw_queries(key, part):
    shape = (BATCH, DRAFT, QHEADS * ATT_DIM)
    base = jnp.clip(jax.random.normal(jax.random.fold_in(key, 11), shape), -4.0, 4.0)
    return base.astype(jnp.bfloat16)


def draw_cached_key_rows(key, part):
    shape = (BATCH, CACHE, KVHEADS * ATT_DIM)
    base = jnp.clip(jax.random.normal(jax.random.fold_in(key, 21), shape), -4.0, 4.0)
    return base.astype(jnp.bfloat16)


def with_ends(result, rng, low, top_value):
    shape = result.shape
    place = [jax.random.randint(jax.random.fold_in(rng, axis), (), 0, shape[axis]) for axis in range(len(shape))]
    result = result.at[tuple(place)].set(low)
    longest = shape.index(max(shape))
    place[longest] = (place[longest] + 1) % shape[longest]
    return result.at[tuple(place)].set(top_value)


def level_of(key, extent, shards, least, high):
    factor_of = 1.0
    for dim, parts in shards:
        steps = jax.random.uniform(jax.random.fold_in(jax.random.fold_in(key, 6), dim), (parts,), jnp.float32, least / len(shards), high / len(shards))
        factor_of = factor_of * jnp.repeat(jnp.exp(steps), extent[dim] // parts).reshape((-1,) + (1,) * (len(extent) - 1 - dim))
    return factor_of


def scatter_about(rng, shape, deviation, bound, cuts=(), dtype=jnp.bfloat16):
    values = deviation * jax.random.normal(rng, shape, jnp.float32)
    if cuts:
        values = values * level_of(rng, shape, cuts, -0.22, 0.18)
    return jnp.clip(values, -bound, bound).astype(dtype)


def setup_inputs(seed: int = 0) -> dict:
    key_of = jax.random.split(jax.random.key(seed), 18)
    return {
        "mamba_input": scatter_about(key_of[0], (BATCH, DRAFT, HEADS * HEAD_DIM), 1.0, 6.0, ((0, 16), (1, 4), (2, 8))),
        "gate_input": scatter_about(key_of[1], (BATCH, DRAFT, HEADS * HEAD_DIM), 1.0, 6.0, ((0, 16), (1, 4), (2, 8))),
        "in_b": scatter_about(key_of[2], (BATCH, DRAFT, GROUPS * STATE), 0.125, 0.75, ((0, 16), (1, 4), (2, 8))),
        "in_c": scatter_about(key_of[3], (BATCH, DRAFT, GROUPS * STATE), 0.125, 0.75, ((0, 16), (1, 4), (2, 8))),
        "step_size": jnp.clip(jnp.exp(math.log(1.0) - 3.9171631 * jax.random.uniform(key_of[4], (BATCH, DRAFT, HEADS), jnp.float32) ** level_of(key_of[4], (BATCH, DRAFT, HEADS), ((0, 16), (1, 4), (2, 8)), -0.2, 0.2)), 0.019897461, 1.0).astype(jnp.bfloat16),
        "decay_rate": jnp.clip(jnp.exp(math.log(1.0) - 4.6051702 * jax.random.uniform(key_of[5], (HEADS,), jnp.float32) ** level_of(key_of[5], (HEADS,), ((0, 8),), -0.2, 0.2)), 0.01, 1.0),
        "skip_weight": jnp.clip(0.5 + 1.0 * jax.random.uniform(key_of[6], (HEADS,), jnp.float32) ** level_of(key_of[6], (HEADS,), ((0, 8),), -0.2, 0.2), 0.5, 1.5),
        "norm_gain": jnp.clip(1.0 + 0.18 * jax.random.normal(key_of[7], (HEADS * HEAD_DIM,), jnp.float32), 0.1, 1.9),
        "ssm_state": scatter_about(key_of[8], (BATCH, HEADS, HEAD_DIM, STATE), 1.0, 6.0, ((0, 16), (1, 8), (3, 4))),
        "out_weight": scatter_about(key_of[9], (HEADS * HEAD_DIM, D), (HEADS * HEAD_DIM) ** -0.5, 0.0625, ((0, 32),)),
        "queries": draw_queries(jax.random.fold_in(key_of[17], 71), 0),
        "draft_token_keys": scatter_about(key_of[11], (BATCH, DRAFT, KVHEADS * ATT_DIM), 1.0, 6.0, ((0, 16), (1, 4), (2, 8))),
        "draft_values": scatter_about(key_of[12], (BATCH, DRAFT, KVHEADS * ATT_DIM), 1.0, 6.0, ((0, 16), (1, 4), (2, 8))),
        "cached_key_rows": draw_cached_key_rows(jax.random.fold_in(key_of[17], 71), 0),
        "cache_values": scatter_about(key_of[14], (BATCH, CACHE, KVHEADS * ATT_DIM), 1.0, 6.0, ((0, 16), (1, 4), (2, 8))),
        "cache_len": with_ends(jax.random.randint(key_of[15], (BATCH,), 2, CACHE + 1), jax.random.fold_in(key_of[15], 1), 2, CACHE).astype(jnp.int32),
        "accepted": with_ends(jax.random.randint(key_of[16], (BATCH,), 0, DRAFT + 1), jax.random.fold_in(key_of[16], 1), 0, DRAFT).astype(jnp.int32),
    }


PRECISE = lax.Precision.HIGHEST
EPSILON = 1e-05
MASKED = -1e+30

def attend_one(inputs):
    query_matrix, new_keys, new_values, old_keys, old_values, valid_length = inputs
    draft_len = query_matrix.shape[0]
    kv_heads = new_keys.shape[1] // ATT_DIM
    per_kv = query_matrix.shape[1] // ATT_DIM // kv_heads
    cache_size = old_keys.shape[0]
    queries_f = query_matrix.astype(jnp.float32).reshape(draft_len, kv_heads, per_kv, ATT_DIM)
    keys_f = jnp.concatenate([old_keys, new_keys], axis=0).astype(jnp.float32).reshape(cache_size + draft_len, kv_heads, ATT_DIM)
    values_f = jnp.concatenate([old_values, new_values], axis=0).astype(jnp.float32).reshape(cache_size + draft_len, kv_heads, ATT_DIM)
    scores = jnp.einsum('sgqd,kgd->gsqk', queries_f, keys_f, precision=PRECISE) * ATT_DIM ** (-0.5)
    key_pos = jnp.arange(cache_size + draft_len)
    query_pos = jnp.arange(draft_len)
    allowed = jnp.where(key_pos[None, :] < cache_size, key_pos[None, :] < valid_length, key_pos[None, :] - cache_size <= query_pos[:, None])
    allowed = allowed[None, :, None, :]
    scores = jnp.where(allowed, scores, MASKED)
    row_peak = lax.optimization_barrier(jnp.max(scores, axis=-1, keepdims=True))
    probs = jnp.where(allowed, jnp.exp(scores - row_peak), 0.0)
    totals = lax.optimization_barrier(jnp.sum(probs, axis=-1))
    rounded = lax.optimization_barrier(probs.astype(jnp.bfloat16)).astype(jnp.float32)
    numer = jnp.einsum('gsqk,kgd->gsqd', rounded, values_f, precision=PRECISE)
    context = numer / totals[..., None]
    return jnp.transpose(context, (1, 0, 2, 3)).reshape(draft_len, kv_heads * per_kv * ATT_DIM).astype(jnp.bfloat16)

def reference(mamba_input, gate_input, in_b, in_c, step_size, decay_rate, skip_weight, norm_gain, ssm_state, out_weight, queries, draft_token_keys, draft_values, cached_key_rows, cache_values, cache_len, accepted):
    batch, draft_len, feature_width = mamba_input.shape
    head_count = decay_rate.shape[0]
    group_count = in_b.shape[2] // STATE
    per_group = head_count // group_count
    feature_values = mamba_input.astype(jnp.float32).reshape(batch, draft_len, head_count, HEAD_DIM)
    step_sizes = step_size.astype(jnp.float32)
    inflow = jnp.repeat(in_b.astype(jnp.float32).reshape(batch, draft_len, group_count, STATE), per_group, axis=2)
    readout = jnp.repeat(in_c.astype(jnp.float32).reshape(batch, draft_len, group_count, STATE), per_group, axis=2)
    log_decay = -step_sizes * decay_rate[None, None, :]
    running = jnp.cumsum(log_decay, axis=1)
    position = jnp.arange(draft_len)
    causal = (position[:, None] >= position[None, :])[None, :, :, None]
    log_gaps = jnp.where(causal, running[:, :, None, :] - running[:, None, :, :], 0.0)
    decays = jnp.where(causal, jnp.exp(log_gaps), 0.0)
    affinity = jnp.einsum('bshn,brhn->bsrh', readout, inflow, precision=PRECISE)
    mixing = affinity * decays * step_sizes[:, None, :, :]
    within = jnp.einsum('bsrh,brhp->bshp', mixing, feature_values, precision=PRECISE)
    start_state = ssm_state.astype(jnp.float32)
    carried = jnp.einsum('bshn,bhpn->bshp', readout, start_state, precision=PRECISE) * jnp.exp(running)[..., None]
    mixed = within + carried + skip_weight[None, None, :, None] * feature_values
    gated = mixed.reshape(batch, draft_len, feature_width) * jax.nn.silu(gate_input.astype(jnp.float32))
    grouped = gated.reshape(batch, draft_len, group_count, feature_width // group_count)
    mean_sq = lax.optimization_barrier(jnp.mean(grouped * grouped, axis=-1, keepdims=True))
    normed = (grouped * lax.rsqrt(mean_sq + EPSILON)).reshape(batch, draft_len, feature_width) * norm_gain
    normed = normed.astype(jnp.bfloat16)
    blocks = N_HEAD * N_TOK
    block_rows = feature_width // blocks
    pieces = jnp.transpose(normed.reshape(batch * draft_len, blocks, block_rows), (1, 0, 2))
    weight_blocks = out_weight.reshape(blocks, block_rows, out_weight.shape[1])

    def add_block(accum, pair):
        piece, weight = pair
        part_sum = jnp.dot(piece, weight, preferred_element_type=jnp.float32)
        part_sum = lax.optimization_barrier(part_sum.astype(jnp.bfloat16)).astype(jnp.float32)
        return (accum + part_sum, None)
    summed_total, unused = lax.scan(add_block, jnp.zeros((batch * draft_len, out_weight.shape[1]), jnp.float32), (pieces, weight_blocks))
    mamba_out = jnp.transpose(summed_total.reshape(batch, draft_len, out_weight.shape[1]), (1, 0, 2)).astype(jnp.bfloat16)
    alive = (position[None, :] < accepted[:, None])[..., None]
    end_log = lax.optimization_barrier(jnp.sum(jnp.where(alive, log_decay, 0.0), axis=1))
    weights = jnp.where(alive, jnp.exp(jnp.where(alive, end_log[:, None, :] - running, 0.0)) * step_sizes, 0.0)
    committed = jnp.exp(end_log)[..., None, None] * start_state + jnp.einsum('bsh,bshp,bshn->bhpn', weights, feature_values, inflow, precision=PRECISE)
    committed_state = committed.astype(jnp.bfloat16)
    attn_context = lax.map(attend_one, (queries, draft_token_keys, draft_values, cached_key_rows, cache_values, cache_len))
    return (mamba_out, attn_context, committed_state)
```

```python
import functools

import jax
import jax.numpy as jnp
from jax import lax
from jax.experimental import pallas as pl
from jax.experimental.pallas import tpu as pltpu
from jax.sharding import PartitionSpec as P

EPSILON = 1e-05
MASKED = -1e30
FLOOR = -1e20
INTERPRET = False

F32 = jnp.float32
BF16 = jnp.bfloat16

X_ROW = 0
Z_ROW = 64
B_ROW = 128
C_ROW = 160
Q_ROW = 192
S_ROW = 320
T_ROW = 448
ROWS = 480

N_ROW = 0
M_ROW = 128
H_ROW = 256
BACK_ROWS = 384

HALF = 2048
WIDTH = HALF + 128


def dot(a, b):
    return jnp.dot(a, b, preferred_element_type=F32)


def dot_t(a, b):
    return lax.dot_general(a, b, (((1,), (1,)), ((), ())), preferred_element_type=F32)


def iota(shape, dim):
    return lax.broadcasted_iota(jnp.int32, shape, dim)


def pack_kernel(x_ref, z_ref, b_ref, c_ref, t_ref, s_ref, q_ref, out_ref):
    for seq in range(2):
        bs = b_ref[seq]
        cs = c_ref[seq]
        steps = t_ref[seq]
        for to in range(4):
            for block in range(2):
                lanes = pl.ds(to * 256 + block * 128, 128)
                row = (seq * 2 + block) * 16
                out_ref[to, pl.ds(X_ROW + row, 16), :] = x_ref[seq, :, lanes]
                out_ref[to, pl.ds(Z_ROW + row, 16), :] = z_ref[seq, :, lanes]
                head = to * 4 + block * 2
                pair = jnp.concatenate([s_ref[seq, head], s_ref[seq, head + 1]], axis=1)
                out_ref[to, pl.ds(S_ROW + (seq * 2 + block) * 32, 32), :] = pair
            out_ref[to, pl.ds(B_ROW + seq * 16, 16), :] = bs
            out_ref[to, pl.ds(C_ROW + seq * 16, 16), :] = cs
            for head in range(4):
                row = Q_ROW + (seq * 4 + head) * 16
                out_ref[to, pl.ds(row, 16), :] = q_ref[seq, :, pl.ds(head * 128, 128)]
            own = steps[:, to * 4 : to * 4 + 4].astype(F32)
            own = jnp.concatenate([own, jnp.zeros((16, 124), F32)], axis=1)
            out_ref[to, pl.ds(T_ROW + seq * 16, 16), :] = own.astype(BF16)


def both(in_ref, first, stride):
    return jnp.concatenate(
        [in_ref[src, pl.ds(first + seq * stride, 16), :] for seq in range(2) for src in range(4)],
        axis=0,
    )


def mixer_kernel(
    in_ref, w_ref, rate_ref, skip_ref, gain_ref, out_ref, run_ref, w_buf, sem
):
    fetch = pltpu.make_async_copy(w_ref, w_buf, sem)
    fetch.start()
    row = iota((128, 128), 0)
    col = iota((128, 128), 1)
    low = col < 64
    causal = (row >= col) & ((row >= 64) == (col >= 64))
    ones = jnp.where(causal, 1.0, 0.0).astype(BF16)
    steps = both(in_ref, T_ROW, 16)
    total = dot(ones, steps)
    rate = rate_ref[...]
    run = -total * rate
    run_ref[...] = run
    run_t = run.T
    steps_t = steps.astype(F32).T
    grow = jnp.exp(run)
    inflow = both(in_ref, B_ROW, 16)
    readout = both(in_ref, C_ROW, 16)
    affinity = dot_t(readout, inflow)
    squares = jnp.zeros((128, 1), F32)
    parts = []
    for block in range(2):
        x = both(in_ref, X_ROW + block * 16, 32)
        z = both(in_ref, Z_ROW + block * 16, 32).astype(F32)
        mixed = []
        for half in range(2):
            head = block * 2 + half
            gap = jnp.where(causal, run[:, head : head + 1] - run_t[head : head + 1, :], 0.0)
            mixing = jnp.where(
                causal, jnp.exp(gap) * steps_t[head : head + 1, :] * affinity, 0.0
            )
            mixed.append(dot(mixing.astype(BF16), x))
        y = jnp.where(low, mixed[0], mixed[1])
        carried = []
        for seq in range(2):
            state = jnp.concatenate(
                [
                    in_ref[src, pl.ds(S_ROW + (seq * 2 + block) * 32, 32), :]
                    for src in range(4)
                ],
                axis=0,
            )
            carried.append(dot(readout[seq * 64 : seq * 64 + 64], state))
        factor = jnp.where(
            low, grow[:, 2 * block : 2 * block + 1], grow[:, 2 * block + 1 : 2 * block + 2]
        )
        lanes = pl.ds(block * 128, 128)
        y = y + jnp.concatenate(carried, axis=0) * factor + skip_ref[:, lanes] * x.astype(F32)
        gated = y * (z / (1.0 + jnp.exp(-z)))
        squares = squares + jnp.sum(gated * gated, axis=1, keepdims=True)
        parts.append((gated * gain_ref[:, lanes]).astype(BF16))
    act = jnp.concatenate(parts, axis=1)
    first = jnp.where(col == (row % 2) * 64 + row // 2, 1.0, 0.0).astype(BF16)
    other = (row // 8) * 8 + (row + 4) % 8
    second = jnp.where(col == (other % 2) * 64 + other // 2, 1.0, 0.0).astype(BF16)
    lhs_a = dot(first, act).astype(BF16)
    lhs_b = dot(second, act).astype(BF16)
    squares = jnp.broadcast_to(squares, (128, 128)).astype(BF16)

    def store(a, b, lanes, width):
        a = a.reshape(16, 8, width)
        b = b.reshape(16, 8, width)
        upper = iota((16, 8, width), 1) < 4
        even = jnp.where(upper, a, b)
        odd = jnp.where(upper, b, a)
        out_ref[:, :, lanes] = jnp.stack([even, odd], axis=1).reshape(32, 8, width).astype(BF16)

    store(dot(first, squares), dot(second, squares), pl.ds(HALF, 128), 128)
    fetch.wait()
    for chunk in range(8):
        lanes = pl.ds(chunk * 256, 256)
        a = dot(lhs_a, w_buf[:, lanes])
        b = dot(lhs_b, w_buf[:, pl.ds(HALF + chunk * 256, 256)])
        store(a, b, lanes, 256)


def attend_kernel(
    where_ref, len_ref, acc_ref, in_ref, run_ref, rate_ref, k_ref, v_ref, dk_ref, dv_ref, out_ref
):
    tok = where_ref[0]
    scale = 128 ** (-0.5)
    cache = k_ref.shape[1]
    for seq in range(2):
        queries = jnp.concatenate(
            [in_ref[src, pl.ds(Q_ROW + seq * 64, 64), :] for src in range(4)], axis=0
        )
        old = dot_t(queries, k_ref[seq]) * scale
        new = dot_t(queries, dk_ref[seq]) * scale
        limit = len_ref[seq] - tok * cache
        old = jnp.where(iota(old.shape, 1) < limit, old, MASKED)
        line = iota(new.shape, 0)
        draft = (line // 64) * 16 + line % 16
        new = jnp.where(iota(new.shape, 1) + tok * 16 <= draft, new, MASKED)
        peak = jnp.maximum(
            jnp.max(old, axis=1, keepdims=True), jnp.max(new, axis=1, keepdims=True)
        )
        peak = jnp.maximum(peak, FLOOR).astype(BF16).astype(F32)
        old = jnp.exp(old - peak)
        new = jnp.exp(new - peak)
        total = jnp.sum(old, axis=1, keepdims=True) + jnp.sum(new, axis=1, keepdims=True)
        numer = dot(old.astype(BF16), v_ref[seq]) + dot(new.astype(BF16), dv_ref[seq])
        numer = numer.astype(BF16)
        stats = jnp.where(iota((256, 128), 1) < 64, peak, total).astype(BF16)
        for to in range(4):
            out_ref[to, pl.ds(N_ROW + seq * 64, 64), :] = numer[to * 64 : to * 64 + 64]
            out_ref[to, pl.ds(M_ROW + seq * 64, 64), :] = stats[to * 64 : to * 64 + 64]

    row = iota((128, 128), 0)
    low = iota((128, 128), 1) < 64
    low_row = iota((1, 128), 1) < 64
    steps = both(in_ref, T_ROW, 16).astype(F32)
    inflow_t = both(in_ref, B_ROW, 16).astype(F32).T.astype(BF16)
    run = run_ref[...]
    rate = rate_ref[...]
    for seq in range(2):
        alive = (row >= seq * 64) & (row < seq * 64 + acc_ref[seq])
        end = -jnp.sum(jnp.where(alive, steps, 0.0), axis=0, keepdims=True) * rate
        weights = jnp.where(alive, jnp.exp(jnp.where(alive, end - run, 0.0)) * steps, 0.0)
        keep = jnp.exp(end)
        for block in range(2):
            first, second = 2 * block, 2 * block + 1
            x = both(in_ref, X_ROW + block * 16, 32).astype(F32)
            factor = jnp.where(
                low, weights[:, first : first + 1], weights[:, second : second + 1]
            )
            added = dot(inflow_t, (x * factor).astype(BF16))
            decay = jnp.where(low_row, keep[:, first : first + 1], keep[:, second : second + 1])
            for src in range(4):
                at = (seq * 2 + block) * 32
                state = in_ref[src, pl.ds(S_ROW + at, 32), :].astype(F32)
                result = decay * state + added[src * 32 : src * 32 + 32]
                out_ref[src, pl.ds(H_ROW + at, 32), :] = result.astype(BF16)


def combine_kernel(in_ref, att_ref, state_ref):
    for seq in range(2):
        stats = [in_ref[src, pl.ds(M_ROW + seq * 64, 64), :].astype(F32) for src in range(4)]
        peaks = [s[:, 0:1] for s in stats]
        overall = functools.reduce(jnp.maximum, peaks)
        numer = jnp.zeros((64, 128), F32)
        denominator = jnp.zeros((64, 1), F32)
        for src in range(4):
            rescale = jnp.exp(peaks[src] - overall)
            denominator = denominator + rescale * stats[src][:, 64:65]
            part = in_ref[src, pl.ds(N_ROW + seq * 64, 64), :].astype(F32)
            numer = numer + rescale * part
        context = (numer / denominator).astype(BF16)
        for head in range(4):
            att_ref[seq, :, pl.ds(head * 128, 128)] = context[head * 16 : head * 16 + 16]
        for src in range(4):
            for block in range(2):
                pair = in_ref[src, pl.ds(H_ROW + (seq * 2 + block) * 32, 32), :]
                state_ref[seq, src * 4 + block * 2] = pair[:, :64]
                state_ref[seq, src * 4 + block * 2 + 1] = pair[:, 64:]


def sum_kernel(where_ref, in_ref, out_ref):
    squares = in_ref[:, :, pl.ds(HALF, 128)].astype(F32)
    squares = squares.reshape(8, 4, 8, 128).sum(axis=1)
    scale = lax.rsqrt(squares * (1.0 / 1024.0) + EPSILON)
    swapped = where_ref[0] % 2 == 1
    for chunk in range(HALF // 128):
        part = in_ref[:, :, pl.ds(chunk * 128, 128)].astype(F32)
        part = part.reshape(8, 4, 8, 128).sum(axis=1)
        total = (part * scale).sum(axis=0)
        flipped = jnp.concatenate([total[4:8], total[0:4]], axis=0)
        total = jnp.where(swapped, flipped, total).astype(BF16)
        for draft in range(2):
            for half in range(2):
                rows = total[half * 4 + draft * 2 : half * 4 + draft * 2 + 2]
                out_ref[draft, :, pl.ds(half * HALF + chunk * 128, 128)] = rows


def in_vmem(count):
    return [pl.BlockSpec(memory_space=pltpu.VMEM) for _ in range(count)]


def in_smem(count):
    return [pl.BlockSpec(memory_space=pltpu.SMEM) for _ in range(count)]


def call(kernel, ins, outs, cost, **kwargs):
    flops, moved = cost
    return pl.pallas_call(
        kernel,
        in_specs=ins,
        out_specs=tuple(in_vmem(len(outs))),
        out_shape=tuple(jax.ShapeDtypeStruct(s, d) for s, d in outs),
        cost_estimate=pl.CostEstimate(flops=flops, bytes_accessed=moved, transcendentals=0),
        interpret=INTERPRET,
        **kwargs,
    )


def body(
    mamba_input,
    gate_input,
    in_b,
    in_c,
    step_size,
    decay_rate,
    skip_weight,
    norm_gain,
    ssm_state,
    out_weight,
    queries,
    draft_token_keys,
    draft_values,
    cached_key_rows,
    cache_values,
    cache_len,
    accepted,
):
    tok = lax.axis_index("tok")
    where = tok.reshape(1).astype(jnp.int32)
    (packed,) = call(pack_kernel, in_vmem(7), [((4, ROWS, 128), BF16)], (0, 1500000))(
        mamba_input,
        gate_input,
        in_b,
        in_c,
        step_size,
        jnp.swapaxes(ssm_state, 2, 3),
        queries,
    )
    arrived = lax.all_to_all(packed, "tok", split_axis=0, concat_axis=0, tiled=True)
    rate = jnp.pad(lax.dynamic_slice(decay_rate, (tok * 4,), (4,)), (0, 124)).reshape(1, 128)
    skip = jnp.repeat(lax.dynamic_slice(skip_weight, (tok * 4,), (4,)), 64).reshape(1, 256)
    gain = lax.dynamic_slice(norm_gain, (tok * 256,), (256,)).reshape(1, 256)
    shares, run = call(
        mixer_kernel,
        in_vmem(1) + [pl.BlockSpec(memory_space=pl.ANY)] + in_vmem(3),
        [((32, 8, WIDTH), BF16), ((128, 128), F32)],
        (400000000, 4000000),
        scratch_shapes=[pltpu.VMEM((256, 4096), BF16), pltpu.SemaphoreType.DMA],
    )(arrived, out_weight, rate, skip, gain)
    landed = lax.all_to_all(shares, ("head", "tok"), split_axis=0, concat_axis=0, tiled=True)
    (back,) = call(
        attend_kernel, in_smem(3) + in_vmem(7), [((4, BACK_ROWS, 128), BF16)], (300000000, 3000000)
    )(
        where,
        cache_len,
        accepted,
        arrived,
        run,
        rate,
        cached_key_rows,
        cache_values,
        draft_token_keys,
        draft_values,
    )
    returned = lax.all_to_all(back, "tok", split_axis=0, concat_axis=0, tiled=True)
    attn_context, state_t = call(
        combine_kernel,
        in_vmem(1),
        [((2, 16, 512), BF16), ((2, 16, 32, 64), BF16)],
        (1000000, 1000000),
    )(returned)
    (mamba_out,) = call(
        sum_kernel, in_smem(1) + in_vmem(1), [((2, 2, 4096), BF16)], (1000000, 1500000)
    )(where, landed)
    return (mamba_out, attn_context, jnp.swapaxes(state_t, 2, 3))


def solution(mesh):
    in_specs = (
        P("dp", "tok", "head"),
        P("dp", "tok", "head"),
        P("dp", "tok", "head"),
        P("dp", "tok", "head"),
        P("dp", "tok", "head"),
        P("head"),
        P("head"),
        P("head"),
        P("dp", "head", None, "tok"),
        P(("head", "tok"), None),
        P("dp", "tok", "head"),
        P("dp", "tok", "head"),
        P("dp", "tok", "head"),
        P("dp", "tok", "head"),
        P("dp", "tok", "head"),
        P("dp"),
        P("dp"),
    )
    out_specs = (
        P(("head", "tok"), "dp", None),
        P("dp", "tok", "head"),
        P("dp", "head", None, "tok"),
    )
    return jax.shard_map(body, mesh=mesh, in_specs=in_specs, out_specs=out_specs, check_vma=False)
```

```python
import functools

import jax
import jax.numpy as jnp
from jax import lax
from jax.experimental import pallas as pl
from jax.experimental.pallas import tpu as pltpu
from jax.sharding import PartitionSpec as P

EPSILON = 1e-05
MASKED = -1e30
FLOOR = -1e20
INTERPRET = False

F32 = jnp.float32
BF16 = jnp.bfloat16

X_ROW = 0
Z_ROW = 64
B_ROW = 128
C_ROW = 160
Q_ROW = 192
S_ROW = 320
T_ROW = 448
ROWS = 480

N_ROW = 0
M_ROW = 128
H_ROW = 256
BACK_ROWS = 384

HALF = 2048
WIDTH = HALF + 128


def dot(a, b):
    return jnp.dot(a, b, preferred_element_type=F32)


def dot_t(a, b):
    return lax.dot_general(a, b, (((1,), (1,)), ((), ())), preferred_element_type=F32)


def iota(shape, dim):
    return lax.broadcasted_iota(jnp.int32, shape, dim)


def pack_kernel(x_ref, z_ref, b_ref, c_ref, t_ref, s_ref, q_ref, out_ref):
    for seq in range(2):
        bs = b_ref[seq]
        cs = c_ref[seq]
        steps = t_ref[seq]
        for to in range(4):
            for block in range(2):
                lanes = pl.ds(to * 256 + block * 128, 128)
                row = (seq * 2 + block) * 16
                out_ref[to, pl.ds(X_ROW + row, 16), :] = x_ref[seq, :, lanes]
                out_ref[to, pl.ds(Z_ROW + row, 16), :] = z_ref[seq, :, lanes]
                head = to * 4 + block * 2
                pair = jnp.concatenate([s_ref[seq, head], s_ref[seq, head + 1]], axis=1)
                out_ref[to, pl.ds(S_ROW + (seq * 2 + block) * 32, 32), :] = pair
            out_ref[to, pl.ds(B_ROW + seq * 16, 16), :] = bs
            out_ref[to, pl.ds(C_ROW + seq * 16, 16), :] = cs
            for head in range(4):
                row = Q_ROW + (seq * 4 + head) * 16
                out_ref[to, pl.ds(row, 16), :] = q_ref[seq, :, pl.ds(head * 128, 128)]
            own = steps[:, to * 4 : to * 4 + 4].astype(F32)
            own = jnp.concatenate([own, jnp.zeros((16, 124), F32)], axis=1)
            out_ref[to, pl.ds(T_ROW + seq * 16, 16), :] = own.astype(BF16)


def both(in_ref, first, stride):
    return jnp.concatenate(
        [in_ref[src, pl.ds(first + seq * stride, 16), :] for seq in range(2) for src in range(4)],
        axis=0,
    )


def mixer_kernel(
    in_ref, w_ref, rate_ref, skip_ref, gain_ref, out_ref, run_ref, w_buf, sem
):
    fetch = pltpu.make_async_copy(w_ref, w_buf, sem)
    fetch.start()
    row = iota((128, 128), 0)
    col = iota((128, 128), 1)
    low = col < 64
    causal = (row >= col) & ((row >= 64) == (col >= 64))
    ones = jnp.where(causal, 1.0, 0.0).astype(BF16)
    steps = both(in_ref, T_ROW, 16)
    total = dot(ones, steps)
    rate = rate_ref[...]
    run = -total * rate
    run_ref[...] = run
    run_t = run.T
    steps_t = steps.astype(F32).T
    grow = jnp.exp(run)
    inflow = both(in_ref, B_ROW, 16)
    readout = both(in_ref, C_ROW, 16)
    affinity = dot_t(readout, inflow)
    squares = jnp.zeros((128, 1), F32)
    parts = []
    for block in range(2):
        x = both(in_ref, X_ROW + block * 16, 32)
        z = both(in_ref, Z_ROW + block * 16, 32).astype(F32)
        mixed = []
        for half in range(2):
            head = block * 2 + half
            gap = jnp.where(causal, run[:, head : head + 1] - run_t[head : head + 1, :], 0.0)
            mixing = jnp.where(
                causal, jnp.exp(gap) * steps_t[head : head + 1, :] * affinity, 0.0
            )
            mixed.append(dot(mixing.astype(BF16), x))
        y = jnp.where(low, mixed[0], mixed[1])
        carried = []
        for seq in range(2):
            state = jnp.concatenate(
                [
                    in_ref[src, pl.ds(S_ROW + (seq * 2 + block) * 32, 32), :]
                    for src in range(4)
                ],
                axis=0,
            )
            carried.append(dot(readout[seq * 64 : seq * 64 + 64], state))
        factor = jnp.where(
            low, grow[:, 2 * block : 2 * block + 1], grow[:, 2 * block + 1 : 2 * block + 2]
        )
        lanes = pl.ds(block * 128, 128)
        y = y + jnp.concatenate(carried, axis=0) * factor + skip_ref[:, lanes] * x.astype(F32)
        gated = y * (z / (1.0 + jnp.exp(-z)))
        squares = squares + jnp.sum(gated * gated, axis=1, keepdims=True)
        parts.append((gated * gain_ref[:, lanes]).astype(BF16))
    act = jnp.concatenate(parts, axis=1)
    first = jnp.where(col == (row % 2) * 64 + row // 2, 1.0, 0.0).astype(BF16)
    other = (row // 8) * 8 + (row + 4) % 8
    second = jnp.where(col == (other % 2) * 64 + other // 2, 1.0, 0.0).astype(BF16)
    lhs_a = dot(first, act).astype(BF16)
    lhs_b = dot(second, act).astype(BF16)
    squares = jnp.broadcast_to(squares, (128, 128)).astype(BF16)

    def store(a, b, lanes, width):
        a = a.reshape(16, 8, width)
        b = b.reshape(16, 8, width)
        upper = iota((16, 8, width), 1) < 4
        even = jnp.where(upper, a, b)
        odd = jnp.where(upper, b, a)
        out_ref[:, :, lanes] = jnp.stack([even, odd], axis=1).reshape(32, 8, width).astype(BF16)

    store(dot(first, squares), dot(second, squares), pl.ds(HALF, 128), 128)
    fetch.wait()
    for chunk in range(8):
        lanes = pl.ds(chunk * 256, 256)
        a = dot(lhs_a, w_buf[:, lanes])
        b = dot(lhs_b, w_buf[:, pl.ds(HALF + chunk * 256, 256)])
        store(a, b, lanes, 256)


def attend_kernel(
    where_ref,
    len_ref,
    acc_ref,
    in_ref,
    run_ref,
    rate_ref,
    k_ref,
    v_ref,
    dk_ref,
    dv_ref,
    near_ref,
    next_ref,
    across_ref,
    last_ref,
    out_ref,
):
    tok = where_ref[0]
    scale = 128 ** (-0.5)
    cache = k_ref.shape[1]
    for seq in range(2):
        queries = jnp.concatenate(
            [in_ref[src, pl.ds(Q_ROW + seq * 64, 64), :] for src in range(4)], axis=0
        )
        old = dot_t(queries, k_ref[seq]) * scale
        new = dot_t(queries, dk_ref[seq]) * scale
        limit = len_ref[seq] - tok * cache
        old = jnp.where(iota(old.shape, 1) < limit, old, MASKED)
        line = iota(new.shape, 0)
        draft = (line // 64) * 16 + line % 16
        new = jnp.where(iota(new.shape, 1) + tok * 16 <= draft, new, MASKED)
        peak = jnp.maximum(
            jnp.max(old, axis=1, keepdims=True), jnp.max(new, axis=1, keepdims=True)
        )
        peak = jnp.maximum(peak, FLOOR).astype(BF16).astype(F32)
        old = jnp.exp(old - peak)
        new = jnp.exp(new - peak)
        total = jnp.sum(old, axis=1, keepdims=True) + jnp.sum(new, axis=1, keepdims=True)
        numer = dot(old.astype(BF16), v_ref[seq]) + dot(new.astype(BF16), dv_ref[seq])
        numer = numer.astype(BF16)
        stats = jnp.where(iota((256, 128), 1) < 64, peak, total).astype(BF16)
        for to in range(4):
            out_ref[to, pl.ds(N_ROW + seq * 64, 64), :] = numer[to * 64 : to * 64 + 64]
            out_ref[to, pl.ds(M_ROW + seq * 64, 64), :] = stats[to * 64 : to * 64 + 64]

    row = iota((128, 128), 0)
    low = iota((128, 128), 1) < 64
    low_row = iota((1, 128), 1) < 64
    steps = both(in_ref, T_ROW, 16).astype(F32)
    inflow_t = both(in_ref, B_ROW, 16).astype(F32).T.astype(BF16)
    run = run_ref[...]
    rate = rate_ref[...]
    for seq in range(2):
        alive = (row >= seq * 64) & (row < seq * 64 + acc_ref[seq])
        end = -jnp.sum(jnp.where(alive, steps, 0.0), axis=0, keepdims=True) * rate
        weights = jnp.where(alive, jnp.exp(jnp.where(alive, end - run, 0.0)) * steps, 0.0)
        keep = jnp.exp(end)
        for block in range(2):
            first, second = 2 * block, 2 * block + 1
            x = both(in_ref, X_ROW + block * 16, 32).astype(F32)
            factor = jnp.where(
                low, weights[:, first : first + 1], weights[:, second : second + 1]
            )
            added = dot(inflow_t, (x * factor).astype(BF16))
            decay = jnp.where(low_row, keep[:, first : first + 1], keep[:, second : second + 1])
            for src in range(4):
                at = (seq * 2 + block) * 32
                state = in_ref[src, pl.ds(S_ROW + at, 32), :].astype(F32)
                result = decay * state + added[src * 32 : src * 32 + 32]
                out_ref[src, pl.ds(H_ROW + at, 32), :] = result.astype(BF16)
    for shift, ref in enumerate((near_ref, next_ref, across_ref, last_ref)):
        ref[...] = out_ref[lax.rem(tok + shift, 4)]


def combine_kernel(where_ref, near_ref, next_ref, across_ref, last_ref, att_ref, state_ref):
    refs = (near_ref, next_ref, across_ref, last_ref)
    for seq in range(2):
        stats = [ref[pl.ds(M_ROW + seq * 64, 64), :].astype(F32) for ref in refs]
        peaks = [s[:, 0:1] for s in stats]
        overall = functools.reduce(jnp.maximum, peaks)
        numer = jnp.zeros((64, 128), F32)
        denominator = jnp.zeros((64, 1), F32)
        for ref, peak, stat in zip(refs, peaks, stats):
            rescale = jnp.exp(peak - overall)
            denominator = denominator + rescale * stat[:, 64:65]
            part = ref[pl.ds(N_ROW + seq * 64, 64), :].astype(F32)
            numer = numer + rescale * part
        context = (numer / denominator).astype(BF16)
        for head in range(4):
            att_ref[seq, :, pl.ds(head * 128, 128)] = context[head * 16 : head * 16 + 16]
        for shift, ref in enumerate(refs):
            src = lax.rem(where_ref[0] + 4 - shift, 4)
            for block in range(2):
                pair = ref[pl.ds(H_ROW + (seq * 2 + block) * 32, 32), :]
                state_ref[seq, src * 4 + block * 2] = pair[:, :64]
                state_ref[seq, src * 4 + block * 2 + 1] = pair[:, 64:]


def sum_kernel(where_ref, in_ref, out_ref):
    squares = in_ref[:, :, pl.ds(HALF, 128)].astype(F32)
    squares = squares.reshape(8, 4, 8, 128).sum(axis=1)
    scale = lax.rsqrt(squares * (1.0 / 1024.0) + EPSILON)
    swapped = where_ref[0] % 2 == 1
    for chunk in range(HALF // 128):
        part = in_ref[:, :, pl.ds(chunk * 128, 128)].astype(F32)
        part = part.reshape(8, 4, 8, 128).sum(axis=1)
        total = (part * scale).sum(axis=0)
        flipped = jnp.concatenate([total[4:8], total[0:4]], axis=0)
        total = jnp.where(swapped, flipped, total).astype(BF16)
        for draft in range(2):
            for half in range(2):
                rows = total[half * 4 + draft * 2 : half * 4 + draft * 2 + 2]
                out_ref[draft, :, pl.ds(half * HALF + chunk * 128, 128)] = rows


def in_vmem(count):
    return [pl.BlockSpec(memory_space=pltpu.VMEM) for _ in range(count)]


def in_smem(count):
    return [pl.BlockSpec(memory_space=pltpu.SMEM) for _ in range(count)]


def held(array):
    if INTERPRET:
        return array
    return pltpu.with_memory_space_constraint(array, pltpu.VMEM)


def call(kernel, ins, outs, cost, **kwargs):
    flops, moved = cost
    return pl.pallas_call(
        kernel,
        in_specs=ins,
        out_specs=tuple(in_vmem(len(outs))),
        out_shape=tuple(
            (jax.ShapeDtypeStruct if plain else pltpu.VMEM)(s, d) for s, d, plain in outs
        ),
        cost_estimate=pl.CostEstimate(flops=flops, bytes_accessed=moved, transcendentals=0),
        interpret=INTERPRET,
        **kwargs,
    )


def body(
    mamba_input,
    gate_input,
    in_b,
    in_c,
    step_size,
    decay_rate,
    skip_weight,
    norm_gain,
    ssm_state,
    out_weight,
    queries,
    draft_token_keys,
    draft_values,
    cached_key_rows,
    cache_values,
    cache_len,
    accepted,
):
    tok = lax.axis_index("tok")
    where = tok.reshape(1).astype(jnp.int32)
    (packed,) = call(pack_kernel, in_vmem(7), [((4, ROWS, 128), BF16, INTERPRET)], (0, 1500000))(
        mamba_input,
        gate_input,
        in_b,
        in_c,
        step_size,
        jnp.swapaxes(ssm_state, 2, 3),
        queries,
    )
    arrived = lax.all_to_all(packed, "tok", split_axis=0, concat_axis=0, tiled=True)
    arrived = held(arrived)
    rate = jnp.pad(lax.dynamic_slice(decay_rate, (tok * 4,), (4,)), (0, 124)).reshape(1, 128)
    skip = jnp.repeat(lax.dynamic_slice(skip_weight, (tok * 4,), (4,)), 64).reshape(1, 256)
    gain = lax.dynamic_slice(norm_gain, (tok * 256,), (256,)).reshape(1, 256)
    shares, run = call(
        mixer_kernel,
        in_vmem(1) + [pl.BlockSpec(memory_space=pl.ANY)] + in_vmem(3),
        [((32, 8, WIDTH), BF16, INTERPRET), ((128, 128), F32, INTERPRET)],
        (400000000, 4000000),
        scratch_shapes=[pltpu.VMEM((256, 4096), BF16), pltpu.SemaphoreType.DMA],
    )(arrived, out_weight, rate, skip, gain)
    landed = lax.all_to_all(shares, ("head", "tok"), split_axis=0, concat_axis=0, tiled=True)
    back = call(
        attend_kernel,
        in_smem(3) + in_vmem(7),
        [((BACK_ROWS, 128), BF16, INTERPRET)] * 4,
        (0, 0),
        scratch_shapes=[pltpu.VMEM((4, BACK_ROWS, 128), BF16)],
    )(
        where,
        cache_len,
        accepted,
        arrived,
        held(run),
        rate,
        cached_key_rows,
        cache_values,
        draft_token_keys,
        draft_values,
    )
    returned = [held(back[0])] + [
        held(lax.ppermute(back[k], "tok", [(i, (i + k) % 4) for i in range(4)]))
        for k in (1, 2, 3)
    ]
    attn_context, state_t = call(
        combine_kernel,
        in_smem(1) + in_vmem(4),
        [((2, 16, 512), BF16, True), ((2, 16, 32, 64), BF16, True)],
        (0, 0),
    )(where, *returned)
    (mamba_out,) = call(
        sum_kernel, in_smem(1) + in_vmem(1), [((2, 2, 4096), BF16, True)], (1000000, 1500000)
    )(where, held(landed))
    return (mamba_out, attn_context, jnp.swapaxes(state_t, 2, 3))


def solution(mesh):
    in_specs = (
        P("dp", "tok", "head"),
        P("dp", "tok", "head"),
        P("dp", "tok", "head"),
        P("dp", "tok", "head"),
        P("dp", "tok", "head"),
        P("head"),
        P("head"),
        P("head"),
        P("dp", "head", None, "tok"),
        P(("head", "tok"), None),
        P("dp", "tok", "head"),
        P("dp", "tok", "head"),
        P("dp", "tok", "head"),
        P("dp", "tok", "head"),
        P("dp", "tok", "head"),
        P("dp"),
        P("dp"),
    )
    out_specs = (
        P(("head", "tok"), "dp", None),
        P("dp", "tok", "head"),
        P("dp", "head", None, "tok"),
    )
    return jax.shard_map(body, mesh=mesh, in_specs=in_specs, out_specs=out_specs, check_vma=False)
```

```python
import functools

import jax
import jax.numpy as jnp
from jax import lax
from jax.experimental import pallas as pl
from jax.experimental.pallas import tpu as pltpu
from jax.sharding import PartitionSpec as P

EPSILON = 1e-05
MASKED = -1e30
FLOOR = -1e20
INTERPRET = False

F32 = jnp.float32
BF16 = jnp.bfloat16

PAIR = 512

X_ROW = 0
Z_ROW = 128
B_ROW = 256
C_ROW = 288
Q_ROW = 320
S_ROW = 448
T_ROW = 704
ROWS = 736

N_ROW = 0
M_ROW = 128
H_ROW = 256
BACK_ROWS = 384

COLUMNS = 2048
HALF = 1024
WIDTH = HALF + 128
PIECE = 128


def dot(a, b):
    return jnp.dot(a, b, preferred_element_type=F32)


def dot_t(a, b):
    return lax.dot_general(a, b, (((1,), (1,)), ((), ())), preferred_element_type=F32)


def iota(shape, dim):
    return lax.broadcasted_iota(jnp.int32, shape, dim)


def pack_kernel(
    where_ref, x_ref, z_ref, b_ref, c_ref, t_ref, s_ref, q_ref, w_ref, out_ref, piece_ref, sem
):
    tok, core = where_ref[0], where_ref[1]
    rows = pl.ds(pl.multiple_of(core * PIECE, PIECE), PIECE)
    columns = pl.ds(pl.multiple_of((1 - tok % 2) * COLUMNS, COLUMNS), COLUMNS)
    fetch = pltpu.make_async_copy(w_ref.at[rows, columns], piece_ref, sem)
    fetch.start()
    for seq in range(2):
        bs = b_ref[seq]
        cs = c_ref[seq]
        steps = t_ref[seq].astype(F32)
        heads = [q_ref[seq, :, pl.ds(head * 128, 128)] for head in range(4)]
        for pair in range(2):
            own = steps[:, pair * 8 : pair * 8 + 8]
            own = jnp.concatenate([own, jnp.zeros((16, 120), F32)], axis=1).astype(BF16)
            for block in range(4):
                lanes = pl.ds(pair * PAIR + block * 128, 128)
                row = (seq * 4 + block) * 16
                x = x_ref[seq, :, lanes]
                z = z_ref[seq, :, lanes]
                head = pair * 8 + block * 2
                state = jnp.concatenate([s_ref[seq, head], s_ref[seq, head + 1]], axis=1)
                for to in (2 * pair, 2 * pair + 1):
                    out_ref[to, pl.ds(X_ROW + row, 16), :] = x
                    out_ref[to, pl.ds(Z_ROW + row, 16), :] = z
                    out_ref[to, pl.ds(S_ROW + 2 * row, 32), :] = state
            for to in (2 * pair, 2 * pair + 1):
                out_ref[to, pl.ds(B_ROW + seq * 16, 16), :] = bs
                out_ref[to, pl.ds(C_ROW + seq * 16, 16), :] = cs
                out_ref[to, pl.ds(T_ROW + seq * 16, 16), :] = own
                for head in range(4):
                    row = Q_ROW + (seq * 4 + head) * 16
                    out_ref[to, pl.ds(row, 16), :] = heads[head]
    fetch.wait()


def both(in_ref, first, stride):
    return jnp.concatenate(
        [in_ref[src, pl.ds(first + seq * stride, 16), :] for seq in range(2) for src in range(4)],
        axis=0,
    )


def mixer_kernel(
    where_ref,
    in_ref,
    w_ref,
    same_ref,
    other_ref,
    rate_ref,
    skip_ref,
    gain_ref,
    out_ref,
    run_ref,
    w_buf,
    sems,
):
    side, core = where_ref[0] % 2, where_ref[1]
    columns = pl.ds(pl.multiple_of(side * COLUMNS, COLUMNS), COLUMNS)

    def rows(first, count):
        return w_buf.at[pl.ds(pl.multiple_of(first, PIECE), count), :]

    near = (1 - side) * 256
    fetches = [
        pltpu.make_async_copy(w_ref.at[:, columns], rows(side * 256, 256), sems.at[0]),
        pltpu.make_async_copy(same_ref, rows(near + core * PIECE, PIECE), sems.at[1]),
        pltpu.make_async_copy(other_ref, rows(near + (1 - core) * PIECE, PIECE), sems.at[2]),
    ]
    for fetch in fetches:
        fetch.start()
    row = iota((128, 128), 0)
    col = iota((128, 128), 1)
    low = col < 64
    causal = (row >= col) & ((row >= 64) == (col >= 64))
    ones = jnp.where(causal, 1.0, 0.0).astype(BF16)
    steps = both(in_ref, T_ROW, 16)
    total = dot(ones, steps)
    rate = rate_ref[...]
    run = -total * rate
    run_ref[...] = run
    run_t = run.T
    steps_t = steps.astype(F32).T
    grow = jnp.exp(run)
    inflow = both(in_ref, B_ROW, 16)
    readout = both(in_ref, C_ROW, 16)
    affinity = dot_t(readout, inflow)
    squares = jnp.zeros((128, 1), F32)
    parts = []
    for block in range(4):
        x = both(in_ref, X_ROW + block * 16, 64)
        z = both(in_ref, Z_ROW + block * 16, 64).astype(F32)
        mixed = []
        for half in range(2):
            head = block * 2 + half
            gap = jnp.where(causal, run[:, head : head + 1] - run_t[head : head + 1, :], 0.0)
            mixing = jnp.where(
                causal, jnp.exp(gap) * steps_t[head : head + 1, :] * affinity, 0.0
            )
            mixed.append(dot(mixing.astype(BF16), x))
        y = jnp.where(low, mixed[0], mixed[1])
        carried = []
        for seq in range(2):
            state = jnp.concatenate(
                [
                    in_ref[src, pl.ds(S_ROW + (seq * 4 + block) * 32, 32), :]
                    for src in range(4)
                ],
                axis=0,
            )
            carried.append(dot(readout[seq * 64 : seq * 64 + 64], state))
        factor = jnp.where(
            low, grow[:, 2 * block : 2 * block + 1], grow[:, 2 * block + 1 : 2 * block + 2]
        )
        lanes = pl.ds(block * 128, 128)
        y = y + jnp.concatenate(carried, axis=0) * factor + skip_ref[:, lanes] * x.astype(F32)
        gated = y * (z / (1.0 + jnp.exp(-z)))
        squares = squares + jnp.sum(gated * gated, axis=1, keepdims=True)
        parts.append((gated * gain_ref[:, lanes]).astype(BF16))
    act = jnp.concatenate(parts, axis=1)
    first = jnp.where(col == (row % 2) * 64 + row // 2, 1.0, 0.0).astype(BF16)
    other = (row // 8) * 8 + (row + 4) % 8
    second = jnp.where(col == (other % 2) * 64 + other // 2, 1.0, 0.0).astype(BF16)
    lhs_a = dot(first, act).astype(BF16)
    lhs_b = dot(second, act).astype(BF16)
    squares = jnp.broadcast_to(squares, (128, 128)).astype(BF16)

    def store(a, b, lanes, width):
        a = a.reshape(16, 8, width)
        b = b.reshape(16, 8, width)
        upper = iota((16, 8, width), 1) < 4
        even = jnp.where(upper, a, b)
        odd = jnp.where(upper, b, a)
        out_ref[:, :, lanes] = jnp.stack([even, odd], axis=1).reshape(32, 8, width).astype(BF16)

    store(dot(first, squares), dot(second, squares), pl.ds(HALF, 128), 128)
    for fetch in fetches:
        fetch.wait()
    for chunk in range(HALF // 256):
        lanes = pl.ds(chunk * 256, 256)
        a = dot(lhs_a, w_buf[:, lanes])
        b = dot(lhs_b, w_buf[:, pl.ds(HALF + chunk * 256, 256)])
        store(a, b, lanes, 256)


def attend_kernel(
    where_ref,
    len_ref,
    acc_ref,
    in_ref,
    run_ref,
    rate_ref,
    k_ref,
    v_ref,
    dk_ref,
    dv_ref,
    near_ref,
    next_ref,
    across_ref,
    last_ref,
    out_ref,
):
    tok = where_ref[0]
    scale = 128 ** (-0.5)
    cache = k_ref.shape[1]
    for seq in range(2):
        queries = jnp.concatenate(
            [in_ref[src, pl.ds(Q_ROW + seq * 64, 64), :] for src in range(4)], axis=0
        )
        old = dot_t(queries, k_ref[seq]) * scale
        new = dot_t(queries, dk_ref[seq]) * scale
        limit = len_ref[seq] - tok * cache
        old = jnp.where(iota(old.shape, 1) < limit, old, MASKED)
        line = iota(new.shape, 0)
        draft = (line // 64) * 16 + line % 16
        new = jnp.where(iota(new.shape, 1) + tok * 16 <= draft, new, MASKED)
        peak = jnp.maximum(
            jnp.max(old, axis=1, keepdims=True), jnp.max(new, axis=1, keepdims=True)
        )
        peak = jnp.maximum(peak, FLOOR).astype(BF16).astype(F32)
        old = jnp.exp(old - peak)
        new = jnp.exp(new - peak)
        total = jnp.sum(old, axis=1, keepdims=True) + jnp.sum(new, axis=1, keepdims=True)
        numer = dot(old.astype(BF16), v_ref[seq]) + dot(new.astype(BF16), dv_ref[seq])
        numer = numer.astype(BF16)
        stats = jnp.where(iota((256, 128), 1) < 64, peak, total).astype(BF16)
        for to in range(4):
            out_ref[to, pl.ds(N_ROW + seq * 64, 64), :] = numer[to * 64 : to * 64 + 64]
            out_ref[to, pl.ds(M_ROW + seq * 64, 64), :] = stats[to * 64 : to * 64 + 64]

    row = iota((128, 128), 0)
    low = iota((128, 128), 1) < 64
    low_row = iota((1, 128), 1) < 64
    side = tok % 2

    def pick(values, block):
        cols = [
            jnp.where(side == 0, values[:, k : k + 1], values[:, k + 4 : k + 5])
            for k in (2 * block, 2 * block + 1)
        ]
        return jnp.where(low if values.shape[0] > 1 else low_row, cols[0], cols[1])

    steps = both(in_ref, T_ROW, 16).astype(F32)
    inflow_t = both(in_ref, B_ROW, 16).astype(F32).T.astype(BF16)
    run = run_ref[...]
    rate = rate_ref[...]
    for seq in range(2):
        alive = (row >= seq * 64) & (row < seq * 64 + acc_ref[seq])
        end = -jnp.sum(jnp.where(alive, steps, 0.0), axis=0, keepdims=True) * rate
        weights = jnp.where(alive, jnp.exp(jnp.where(alive, end - run, 0.0)) * steps, 0.0)
        keep = jnp.exp(end)
        for block in range(2):
            start = pl.multiple_of((2 * side + block) * 16, 16)
            x = both(in_ref, X_ROW + start, 64).astype(F32)
            added = dot(inflow_t, (x * pick(weights, block)).astype(BF16))
            decay = pick(keep, block)
            for src in range(4):
                first = pl.multiple_of(S_ROW + seq * 128 + 2 * start, 32)
                state = in_ref[src, pl.ds(first, 32), :].astype(F32)
                result = decay * state + added[src * 32 : src * 32 + 32]
                at = H_ROW + (seq * 2 + block) * 32
                out_ref[src, pl.ds(at, 32), :] = result.astype(BF16)
    for shift, ref in enumerate((near_ref, next_ref, across_ref, last_ref)):
        ref[...] = out_ref[lax.rem(tok + shift, 4)]


def combine_kernel(where_ref, near_ref, next_ref, across_ref, last_ref, att_ref, state_ref):
    refs = (near_ref, next_ref, across_ref, last_ref)
    for seq in range(2):
        stats = [ref[pl.ds(M_ROW + seq * 64, 64), :].astype(F32) for ref in refs]
        peaks = [s[:, 0:1] for s in stats]
        overall = functools.reduce(jnp.maximum, peaks)
        numer = jnp.zeros((64, 128), F32)
        denominator = jnp.zeros((64, 1), F32)
        for ref, peak, stat in zip(refs, peaks, stats):
            rescale = jnp.exp(peak - overall)
            denominator = denominator + rescale * stat[:, 64:65]
            part = ref[pl.ds(N_ROW + seq * 64, 64), :].astype(F32)
            numer = numer + rescale * part
        context = (numer / denominator).astype(BF16)
        for head in range(4):
            att_ref[seq, :, pl.ds(head * 128, 128)] = context[head * 16 : head * 16 + 16]
        for shift, ref in enumerate(refs):
            src = lax.rem(where_ref[0] + 4 - shift, 4)
            for block in range(2):
                pair = ref[pl.ds(H_ROW + (seq * 2 + block) * 32, 32), :]
                state_ref[seq, src * 4 + block * 2] = pair[:, :64]
                state_ref[seq, src * 4 + block * 2 + 1] = pair[:, 64:]


def sum_kernel(where_ref, in_ref, out_ref):
    squares = in_ref[:, :, pl.ds(HALF, 128)].astype(F32)
    squares = squares.reshape(8, 4, 8, 128).sum(axis=1)
    scale = lax.rsqrt(squares * (0.5 / 1024.0) + EPSILON)
    swapped = where_ref[0] % 2 == 1
    for chunk in range(HALF // 128):
        part = in_ref[:, :, pl.ds(chunk * 128, 128)].astype(F32)
        part = part.reshape(8, 2, 2, 8, 128).sum(axis=1)
        both_sides = (part * scale[:, None]).sum(axis=0)
        for side in range(2):
            total = both_sides[side]
            flipped = jnp.concatenate([total[4:8], total[0:4]], axis=0)
            total = jnp.where(swapped, flipped, total).astype(BF16)
            for draft in range(2):
                for half in range(2):
                    rows = total[half * 4 + draft * 2 : half * 4 + draft * 2 + 2]
                    first = side * COLUMNS + half * HALF + chunk * 128
                    out_ref[draft, :, pl.ds(first, 128)] = rows


def in_vmem(count):
    return [pl.BlockSpec(memory_space=pltpu.VMEM) for _ in range(count)]


def in_smem(count):
    return [pl.BlockSpec(memory_space=pltpu.SMEM) for _ in range(count)]


def held(array):
    if INTERPRET:
        return array
    return pltpu.with_memory_space_constraint(array, pltpu.VMEM)


def call(kernel, ins, outs, cost, **kwargs):
    flops, moved = cost
    return pl.pallas_call(
        kernel,
        in_specs=ins,
        out_specs=tuple(in_vmem(len(outs))),
        out_shape=tuple(
            (jax.ShapeDtypeStruct if plain else pltpu.VMEM)(s, d) for s, d, plain in outs
        ),
        cost_estimate=pl.CostEstimate(flops=flops, bytes_accessed=moved, transcendentals=0),
        interpret=INTERPRET,
        **kwargs,
    )


def body(
    mamba_input,
    gate_input,
    in_b,
    in_c,
    step_size,
    decay_rate,
    skip_weight,
    norm_gain,
    ssm_state,
    out_weight,
    queries,
    draft_token_keys,
    draft_values,
    cached_key_rows,
    cache_values,
    cache_len,
    accepted,
):
    tok = lax.axis_index("tok")
    where = jnp.stack([tok, lax.axis_index("dp") % 2]).astype(jnp.int32)
    whole = pl.BlockSpec(memory_space=pl.ANY)
    packed, piece = call(
        pack_kernel,
        in_smem(1) + in_vmem(7) + [whole],
        [((4, ROWS, 128), BF16, True), ((PIECE, COLUMNS), BF16, INTERPRET)],
        (0, 2500000),
        scratch_shapes=[pltpu.SemaphoreType.DMA],
    )(
        where,
        mamba_input,
        gate_input,
        in_b,
        in_c,
        step_size,
        jnp.swapaxes(ssm_state, 2, 3),
        queries,
        out_weight,
    )
    same = lax.ppermute(piece, "tok", [(i, i ^ 1) for i in range(4)])
    other = lax.ppermute(same, "dp", [(i, i ^ 1) for i in range(lax.axis_size("dp"))])
    arrived = lax.all_to_all(packed, "tok", split_axis=0, concat_axis=0, tiled=True)
    arrived = held(arrived)
    pair = tok // 2
    rate = jnp.pad(lax.dynamic_slice(decay_rate, (pair * 8,), (8,)), (0, 120)).reshape(1, 128)
    skip = jnp.repeat(lax.dynamic_slice(skip_weight, (pair * 8,), (8,)), 64).reshape(1, PAIR)
    gain = lax.dynamic_slice(norm_gain, (pair * PAIR,), (PAIR,)).reshape(1, PAIR)
    shares, run = call(
        mixer_kernel,
        in_smem(1) + in_vmem(1) + [whole] + in_vmem(5),
        [((32, 8, WIDTH), BF16, True), ((128, 128), F32, INTERPRET)],
        (400000000, 4000000),
        scratch_shapes=[pltpu.VMEM((PAIR, COLUMNS), BF16), pltpu.SemaphoreType.DMA((3,))],
    )(where, arrived, out_weight, held(same), held(other), rate, skip, gain)
    landed = lax.all_to_all(shares, ("head", "tok"), split_axis=0, concat_axis=0, tiled=True)
    back = call(
        attend_kernel,
        in_smem(3) + in_vmem(7),
        [((BACK_ROWS, 128), BF16, INTERPRET)] * 4,
        (0, 0),
        scratch_shapes=[pltpu.VMEM((4, BACK_ROWS, 128), BF16)],
    )(
        where,
        cache_len,
        accepted,
        arrived,
        held(run),
        rate,
        cached_key_rows,
        cache_values,
        draft_token_keys,
        draft_values,
    )
    returned = [held(back[0])] + [
        held(lax.ppermute(back[k], "tok", [(i, (i + k) % 4) for i in range(4)]))
        for k in (1, 2, 3)
    ]
    attn_context, state_t = call(
        combine_kernel,
        in_smem(1) + in_vmem(4),
        [((2, 16, 512), BF16, True), ((2, 16, 32, 64), BF16, True)],
        (0, 0),
    )(where, *returned)
    (mamba_out,) = call(
        sum_kernel, in_smem(1) + in_vmem(1), [((2, 2, 4096), BF16, True)], (1000000, 1500000)
    )(where, held(landed))
    return (mamba_out, attn_context, jnp.swapaxes(state_t, 2, 3))


def solution(mesh):
    in_specs = (
        P("dp", "tok", "head"),
        P("dp", "tok", "head"),
        P("dp", "tok", "head"),
        P("dp", "tok", "head"),
        P("dp", "tok", "head"),
        P("head"),
        P("head"),
        P("head"),
        P("dp", "head", None, "tok"),
        P(("head", "tok"), None),
        P("dp", "tok", "head"),
        P("dp", "tok", "head"),
        P("dp", "tok", "head"),
        P("dp", "tok", "head"),
        P("dp", "tok", "head"),
        P("dp"),
        P("dp"),
    )
    out_specs = (
        P(("head", "tok"), "dp", None),
        P("dp", "tok", "head"),
        P("dp", "head", None, "tok"),
    )
    return jax.shard_map(body, mesh=mesh, in_specs=in_specs, out_specs=out_specs, check_vma=False)
```

```python
import functools

import jax
import jax.numpy as jnp
from jax import lax
from jax.experimental import pallas as pl
from jax.experimental.pallas import tpu as pltpu
from jax.sharding import PartitionSpec as P

EPSILON = 1e-05
MASKED = -1e30
FLOOR = -1e20
INTERPRET = False

F32 = jnp.float32
BF16 = jnp.bfloat16

X_ROW = 0
Z_ROW = 64
B_ROW = 128
C_ROW = 160
Q_ROW = 192
S_ROW = 320
T_ROW = 448
ROWS = 480

N_ROW = 0
M_ROW = 128
H_ROW = 256
BACK_ROWS = 384

HALF = 2048
WIDTH = HALF + 128


def dot(a, b):
    return jnp.dot(a, b, preferred_element_type=F32)


def dot_t(a, b):
    return lax.dot_general(a, b, (((1,), (1,)), ((), ())), preferred_element_type=F32)


def iota(shape, dim):
    return lax.broadcasted_iota(jnp.int32, shape, dim)


def pack_kernel(x_ref, z_ref, b_ref, c_ref, t_ref, s_ref, q_ref, out_ref):
    for seq in range(2):
        bs = b_ref[seq]
        cs = c_ref[seq]
        steps = t_ref[seq]
        for to in range(4):
            for block in range(2):
                lanes = pl.ds(to * 256 + block * 128, 128)
                row = (seq * 2 + block) * 16
                out_ref[to, pl.ds(X_ROW + row, 16), :] = x_ref[seq, :, lanes]
                out_ref[to, pl.ds(Z_ROW + row, 16), :] = z_ref[seq, :, lanes]
                head = to * 4 + block * 2
                pair = jnp.concatenate([s_ref[seq, head], s_ref[seq, head + 1]], axis=1)
                out_ref[to, pl.ds(S_ROW + (seq * 2 + block) * 32, 32), :] = pair
            out_ref[to, pl.ds(B_ROW + seq * 16, 16), :] = bs
            out_ref[to, pl.ds(C_ROW + seq * 16, 16), :] = cs
            for head in range(4):
                row = Q_ROW + (seq * 4 + head) * 16
                out_ref[to, pl.ds(row, 16), :] = q_ref[seq, :, pl.ds(head * 128, 128)]
            own = steps[:, to * 4 : to * 4 + 4].astype(F32)
            own = jnp.concatenate([own, jnp.zeros((16, 124), F32)], axis=1)
            out_ref[to, pl.ds(T_ROW + seq * 16, 16), :] = own.astype(BF16)


def both(in_ref, first, stride):
    return jnp.concatenate(
        [in_ref[src, pl.ds(first + seq * stride, 16), :] for seq in range(2) for src in range(4)],
        axis=0,
    )


def mixer_kernel(
    in_ref, w_ref, rate_ref, skip_ref, gain_ref, out_ref, run_ref, w_buf, sem
):
    fetch = pltpu.make_async_copy(w_ref, w_buf, sem)
    fetch.start()
    row = iota((128, 128), 0)
    col = iota((128, 128), 1)
    low = col < 64
    causal = (row >= col) & ((row >= 64) == (col >= 64))
    ones = jnp.where(causal, 1.0, 0.0).astype(BF16)
    steps = both(in_ref, T_ROW, 16)
    total = dot(ones, steps)
    rate = rate_ref[...]
    run = -total * rate
    run_ref[...] = run
    run_t = run.T
    steps_t = steps.astype(F32).T
    grow = jnp.exp(run)
    inflow = both(in_ref, B_ROW, 16)
    readout = both(in_ref, C_ROW, 16)
    affinity = dot_t(readout, inflow)
    squares = jnp.zeros((128, 1), F32)
    parts = []
    for block in range(2):
        x = both(in_ref, X_ROW + block * 16, 32)
        z = both(in_ref, Z_ROW + block * 16, 32).astype(F32)
        mixed = []
        for half in range(2):
            head = block * 2 + half
            gap = jnp.where(causal, run[:, head : head + 1] - run_t[head : head + 1, :], 0.0)
            mixing = jnp.where(
                causal, jnp.exp(gap) * steps_t[head : head + 1, :] * affinity, 0.0
            )
            mixed.append(dot(mixing.astype(BF16), x))
        y = jnp.where(low, mixed[0], mixed[1])
        carried = []
        for seq in range(2):
            state = jnp.concatenate(
                [
                    in_ref[src, pl.ds(S_ROW + (seq * 2 + block) * 32, 32), :]
                    for src in range(4)
                ],
                axis=0,
            )
            carried.append(dot(readout[seq * 64 : seq * 64 + 64], state))
        factor = jnp.where(
            low, grow[:, 2 * block : 2 * block + 1], grow[:, 2 * block + 1 : 2 * block + 2]
        )
        lanes = pl.ds(block * 128, 128)
        y = y + jnp.concatenate(carried, axis=0) * factor + skip_ref[:, lanes] * x.astype(F32)
        gated = y * (z / (1.0 + jnp.exp(-z)))
        squares = squares + jnp.sum(gated * gated, axis=1, keepdims=True)
        parts.append((gated * gain_ref[:, lanes]).astype(BF16))
    act = jnp.concatenate(parts, axis=1)
    first = jnp.where(col == (row % 2) * 64 + row // 2, 1.0, 0.0).astype(BF16)
    other = (row // 8) * 8 + (row + 4) % 8
    second = jnp.where(col == (other % 2) * 64 + other // 2, 1.0, 0.0).astype(BF16)
    lhs_a = dot(first, act).astype(BF16)
    lhs_b = dot(second, act).astype(BF16)
    squares = jnp.broadcast_to(squares, (128, 128)).astype(BF16)

    def store(a, b, lanes, width):
        a = a.reshape(16, 8, width)
        b = b.reshape(16, 8, width)
        upper = iota((16, 8, width), 1) < 4
        even = jnp.where(upper, a, b)
        odd = jnp.where(upper, b, a)
        rows = jnp.stack([even, odd], axis=1).reshape(8, 4, 8, width).astype(BF16)
        for to in range(4):
            out_ref[to, :, :, lanes] = rows[:, to]

    store(dot(first, squares), dot(second, squares), pl.ds(HALF, 128), 128)
    fetch.wait()
    for chunk in range(8):
        lanes = pl.ds(chunk * 256, 256)
        a = dot(lhs_a, w_buf[:, lanes])
        b = dot(lhs_b, w_buf[:, pl.ds(HALF + chunk * 256, 256)])
        store(a, b, lanes, 256)


def attend_kernel(
    where_ref,
    len_ref,
    acc_ref,
    in_ref,
    run_ref,
    rate_ref,
    k_ref,
    v_ref,
    dk_ref,
    dv_ref,
    near_ref,
    next_ref,
    across_ref,
    last_ref,
    out_ref,
):
    tok = where_ref[0]
    scale = 128 ** (-0.5)
    cache = k_ref.shape[1]
    for seq in range(2):
        queries = jnp.concatenate(
            [in_ref[src, pl.ds(Q_ROW + seq * 64, 64), :] for src in range(4)], axis=0
        )
        old = dot_t(queries, k_ref[seq]) * scale
        new = dot_t(queries, dk_ref[seq]) * scale
        limit = len_ref[seq] - tok * cache
        old = jnp.where(iota(old.shape, 1) < limit, old, MASKED)
        line = iota(new.shape, 0)
        draft = (line // 64) * 16 + line % 16
        new = jnp.where(iota(new.shape, 1) + tok * 16 <= draft, new, MASKED)
        peak = jnp.maximum(
            jnp.max(old, axis=1, keepdims=True), jnp.max(new, axis=1, keepdims=True)
        )
        peak = jnp.maximum(peak, FLOOR).astype(BF16).astype(F32)
        old = jnp.exp(old - peak)
        new = jnp.exp(new - peak)
        total = jnp.sum(old, axis=1, keepdims=True) + jnp.sum(new, axis=1, keepdims=True)
        numer = dot(old.astype(BF16), v_ref[seq]) + dot(new.astype(BF16), dv_ref[seq])
        numer = numer.astype(BF16)
        stats = jnp.where(iota((256, 128), 1) < 64, peak, total).astype(BF16)
        for to in range(4):
            out_ref[to, pl.ds(N_ROW + seq * 64, 64), :] = numer[to * 64 : to * 64 + 64]
            out_ref[to, pl.ds(M_ROW + seq * 64, 64), :] = stats[to * 64 : to * 64 + 64]

    row = iota((128, 128), 0)
    low = iota((128, 128), 1) < 64
    low_row = iota((1, 128), 1) < 64
    steps = both(in_ref, T_ROW, 16).astype(F32)
    inflow_t = both(in_ref, B_ROW, 16).astype(F32).T.astype(BF16)
    run = run_ref[...]
    rate = rate_ref[...]
    for seq in range(2):
        alive = (row >= seq * 64) & (row < seq * 64 + acc_ref[seq])
        end = -jnp.sum(jnp.where(alive, steps, 0.0), axis=0, keepdims=True) * rate
        weights = jnp.where(alive, jnp.exp(jnp.where(alive, end - run, 0.0)) * steps, 0.0)
        keep = jnp.exp(end)
        for block in range(2):
            first, second = 2 * block, 2 * block + 1
            x = both(in_ref, X_ROW + block * 16, 32).astype(F32)
            factor = jnp.where(
                low, weights[:, first : first + 1], weights[:, second : second + 1]
            )
            added = dot(inflow_t, (x * factor).astype(BF16))
            decay = jnp.where(low_row, keep[:, first : first + 1], keep[:, second : second + 1])
            for src in range(4):
                at = (seq * 2 + block) * 32
                state = in_ref[src, pl.ds(S_ROW + at, 32), :].astype(F32)
                result = decay * state + added[src * 32 : src * 32 + 32]
                out_ref[src, pl.ds(H_ROW + at, 32), :] = result.astype(BF16)
    for shift, ref in enumerate((near_ref, next_ref, across_ref, last_ref)):
        ref[...] = out_ref[lax.rem(tok + shift, 4)]


def combine_kernel(where_ref, near_ref, next_ref, across_ref, last_ref, att_ref, state_ref):
    refs = (near_ref, next_ref, across_ref, last_ref)
    for seq in range(2):
        stats = [ref[pl.ds(M_ROW + seq * 64, 64), :].astype(F32) for ref in refs]
        peaks = [s[:, 0:1] for s in stats]
        overall = functools.reduce(jnp.maximum, peaks)
        numer = jnp.zeros((64, 128), F32)
        denominator = jnp.zeros((64, 1), F32)
        for ref, peak, stat in zip(refs, peaks, stats):
            rescale = jnp.exp(peak - overall)
            denominator = denominator + rescale * stat[:, 64:65]
            part = ref[pl.ds(N_ROW + seq * 64, 64), :].astype(F32)
            numer = numer + rescale * part
        context = (numer / denominator).astype(BF16)
        for head in range(4):
            att_ref[seq, :, pl.ds(head * 128, 128)] = context[head * 16 : head * 16 + 16]
        for shift, ref in enumerate(refs):
            src = lax.rem(where_ref[0] + 4 - shift, 4)
            for block in range(2):
                pair = ref[pl.ds(H_ROW + (seq * 2 + block) * 32, 32), :]
                state_ref[seq, src * 4 + block * 2] = pair[:, :64]
                state_ref[seq, src * 4 + block * 2 + 1] = pair[:, 64:]


def stage_kernel(in_ref, after_ref, out_ref):
    squares = in_ref[:, :, :, pl.ds(HALF, 128)].astype(F32).sum(axis=0)
    scale = lax.rsqrt(squares * (1.0 / 1024.0) + EPSILON)
    for chunk in range(HALF // 128):
        lanes = pl.ds(chunk * 128, 128)
        total = in_ref[:, :, :, lanes].astype(F32).sum(axis=0)
        out_ref[:, :, lanes] = (total * scale).astype(BF16)


def sum_kernel(where_ref, in_ref, out_ref):
    swapped = where_ref[0] % 2 == 1
    for chunk in range(HALF // 128):
        total = in_ref[:, :, pl.ds(chunk * 128, 128)].astype(F32).sum(axis=0)
        flipped = jnp.concatenate([total[4:8], total[0:4]], axis=0)
        total = jnp.where(swapped, flipped, total).astype(BF16)
        for draft in range(2):
            for half in range(2):
                rows = total[half * 4 + draft * 2 : half * 4 + draft * 2 + 2]
                out_ref[draft, :, pl.ds(half * HALF + chunk * 128, 128)] = rows


def in_vmem(count):
    return [pl.BlockSpec(memory_space=pltpu.VMEM) for _ in range(count)]


def in_smem(count):
    return [pl.BlockSpec(memory_space=pltpu.SMEM) for _ in range(count)]


def held(array):
    if INTERPRET:
        return array
    return pltpu.with_memory_space_constraint(array, pltpu.VMEM)


def call(kernel, ins, outs, cost, **kwargs):
    flops, moved = cost
    return pl.pallas_call(
        kernel,
        in_specs=ins,
        out_specs=tuple(in_vmem(len(outs))),
        out_shape=tuple(
            (jax.ShapeDtypeStruct if plain else pltpu.VMEM)(s, d) for s, d, plain in outs
        ),
        cost_estimate=pl.CostEstimate(flops=flops, bytes_accessed=moved, transcendentals=0),
        interpret=INTERPRET,
        **kwargs,
    )


def body(
    mamba_input,
    gate_input,
    in_b,
    in_c,
    step_size,
    decay_rate,
    skip_weight,
    norm_gain,
    ssm_state,
    out_weight,
    queries,
    draft_token_keys,
    draft_values,
    cached_key_rows,
    cache_values,
    cache_len,
    accepted,
):
    tok = lax.axis_index("tok")
    where = tok.reshape(1).astype(jnp.int32)
    (packed,) = call(pack_kernel, in_vmem(7), [((4, ROWS, 128), BF16, INTERPRET)], (0, 1500000))(
        mamba_input,
        gate_input,
        in_b,
        in_c,
        step_size,
        jnp.swapaxes(ssm_state, 2, 3),
        queries,
    )
    arrived = lax.all_to_all(packed, "tok", split_axis=0, concat_axis=0, tiled=True)
    arrived = held(arrived)
    rate = jnp.pad(lax.dynamic_slice(decay_rate, (tok * 4,), (4,)), (0, 124)).reshape(1, 128)
    skip = jnp.repeat(lax.dynamic_slice(skip_weight, (tok * 4,), (4,)), 64).reshape(1, 256)
    gain = lax.dynamic_slice(norm_gain, (tok * 256,), (256,)).reshape(1, 256)
    shares, run = call(
        mixer_kernel,
        in_vmem(1) + [pl.BlockSpec(memory_space=pl.ANY)] + in_vmem(3),
        [((4, 8, 8, WIDTH), BF16, INTERPRET), ((128, 128), F32, INTERPRET)],
        (400000000, 4000000),
        scratch_shapes=[pltpu.VMEM((256, 4096), BF16), pltpu.SemaphoreType.DMA],
    )(arrived, out_weight, rate, skip, gain)
    nearer = lax.all_to_all(shares, "tok", split_axis=0, concat_axis=0, tiled=True)
    back = call(
        attend_kernel,
        in_smem(3) + in_vmem(7),
        [((BACK_ROWS, 128), BF16, INTERPRET)] * 4,
        (0, 0),
        scratch_shapes=[pltpu.VMEM((4, BACK_ROWS, 128), BF16)],
    )(
        where,
        cache_len,
        accepted,
        arrived,
        held(run),
        rate,
        cached_key_rows,
        cache_values,
        draft_token_keys,
        draft_values,
    )
    (staged,) = call(
        stage_kernel, in_vmem(2), [((8, 8, HALF), BF16, INTERPRET)], (2000000, 1500000)
    )(held(nearer), held(back[0]))
    landed = lax.all_to_all(staged, "head", split_axis=0, concat_axis=0, tiled=True)
    returned = [held(back[0])] + [
        held(lax.ppermute(back[k], "tok", [(i, (i + k) % 4) for i in range(4)]))
        for k in (1, 2, 3)
    ]
    attn_context, state_t = call(
        combine_kernel,
        in_smem(1) + in_vmem(4),
        [((2, 16, 512), BF16, True), ((2, 16, 32, 64), BF16, True)],
        (0, 0),
    )(where, *returned)
    (mamba_out,) = call(
        sum_kernel, in_smem(1) + in_vmem(1), [((2, 2, 4096), BF16, True)], (1000000, 1500000)
    )(where, held(landed))
    return (mamba_out, attn_context, jnp.swapaxes(state_t, 2, 3))


def solution(mesh):
    in_specs = (
        P("dp", "tok", "head"),
        P("dp", "tok", "head"),
        P("dp", "tok", "head"),
        P("dp", "tok", "head"),
        P("dp", "tok", "head"),
        P("head"),
        P("head"),
        P("head"),
        P("dp", "head", None, "tok"),
        P(("head", "tok"), None),
        P("dp", "tok", "head"),
        P("dp", "tok", "head"),
        P("dp", "tok", "head"),
        P("dp", "tok", "head"),
        P("dp", "tok", "head"),
        P("dp"),
        P("dp"),
    )
    out_specs = (
        P(("head", "tok"), "dp", None),
        P("dp", "tok", "head"),
        P("dp", "head", None, "tok"),
    )
    return jax.shard_map(body, mesh=mesh, in_specs=in_specs, out_specs=out_specs, check_vma=False)
```

```python
import functools

import jax
import jax.numpy as jnp
from jax import lax
from jax.experimental import pallas as pl
from jax.experimental.pallas import tpu as pltpu
from jax.sharding import PartitionSpec as P

EPSILON = 1e-05
MASKED = -1e30
FLOOR = -1e20
INTERPRET = False

F32 = jnp.float32
BF16 = jnp.bfloat16

X_ROW = 0
Z_ROW = 64
B_ROW = 128
C_ROW = 160
Q_ROW = 192
S_ROW = 320
T_ROW = 448
ROWS = 464

N_ROW = 0
M_ROW = 128
H_ROW = 256
BACK_ROWS = 384

HALF = 2048
WIDTH = HALF + 128


def dot(a, b):
    return jnp.dot(a, b, preferred_element_type=F32)


def dot_t(a, b):
    return lax.dot_general(a, b, (((1,), (1,)), ((), ())), preferred_element_type=F32)


def iota(shape, dim):
    return lax.broadcasted_iota(jnp.int32, shape, dim)


def pack_kernel(x_ref, z_ref, b_ref, c_ref, t_ref, s_ref, q_ref, out_ref, buf, sems):
    pad = jnp.zeros((16, 60), F32)
    copies = []
    for to in range(4):
        for seq in range(2):
            for block in range(2):
                lanes = pl.ds(to * 256 + block * 128, 128)
                row = (seq * 2 + block) * 16
                buf[to, pl.ds(X_ROW + row, 16), :] = x_ref[seq, :, lanes]
                buf[to, pl.ds(Z_ROW + row, 16), :] = z_ref[seq, :, lanes]
                head = to * 4 + block * 2
                pair = jnp.concatenate([s_ref[seq, head], s_ref[seq, head + 1]], axis=1)
                buf[to, pl.ds(S_ROW + (seq * 2 + block) * 32, 32), :] = pair
            buf[to, pl.ds(B_ROW + seq * 16, 16), :] = b_ref[seq]
            buf[to, pl.ds(C_ROW + seq * 16, 16), :] = c_ref[seq]
            for head in range(4):
                row = Q_ROW + (seq * 4 + head) * 16
                buf[to, pl.ds(row, 16), :] = q_ref[seq, :, pl.ds(head * 128, 128)]
        own = [t_ref[seq].astype(F32)[:, to * 4 : to * 4 + 4] for seq in range(2)]
        lanes = jnp.concatenate([own[0], pad, own[1], pad], axis=1)
        buf[to, pl.ds(T_ROW, 16), :] = lanes.astype(BF16)
        copy = pltpu.make_async_copy(buf.at[to], out_ref.at[to], sems.at[to])
        copy.start()
        copies.append(copy)
    for copy in copies:
        copy.wait()


def all_steps(in_ref):
    both_lanes = jnp.concatenate(
        [in_ref[src, pl.ds(T_ROW, 16), :].astype(F32) for src in range(4)], axis=0
    )
    swapped = jnp.concatenate([both_lanes[:, 64:], both_lanes[:, :64]], axis=1)
    return jnp.concatenate([both_lanes, swapped], axis=0)


def both(in_ref, first, stride):
    return jnp.concatenate(
        [in_ref[src, pl.ds(first + seq * stride, 16), :] for seq in range(2) for src in range(4)],
        axis=0,
    )


def mixer_kernel(
    in_ref, w_ref, rate_ref, skip_ref, gain_ref, out_ref, run_ref, w_buf, o_buf, sem, out_sems
):
    fetch = pltpu.make_async_copy(w_ref, w_buf, sem)
    fetch.start()
    row = iota((128, 128), 0)
    col = iota((128, 128), 1)
    low = col < 64
    causal = (row >= col) & ((row >= 64) == (col >= 64))
    ones = jnp.where(causal, 1.0, 0.0).astype(BF16)
    steps = all_steps(in_ref)
    total = dot(ones, steps.astype(BF16))
    rate = rate_ref[...]
    run = -total * rate
    run_ref[...] = run
    run_t = run.T
    steps_t = steps.T
    grow = jnp.exp(run)
    inflow = both(in_ref, B_ROW, 16)
    readout = both(in_ref, C_ROW, 16)
    affinity = dot_t(readout, inflow)
    squares = jnp.zeros((128, 1), F32)
    parts = []
    for block in range(2):
        x = both(in_ref, X_ROW + block * 16, 32)
        z = both(in_ref, Z_ROW + block * 16, 32).astype(F32)
        mixed = []
        for half in range(2):
            head = block * 2 + half
            gap = jnp.where(causal, run[:, head : head + 1] - run_t[head : head + 1, :], 0.0)
            mixing = jnp.where(
                causal, jnp.exp(gap) * steps_t[head : head + 1, :] * affinity, 0.0
            )
            mixed.append(dot(mixing.astype(BF16), x))
        y = jnp.where(low, mixed[0], mixed[1])
        carried = []
        for seq in range(2):
            state = jnp.concatenate(
                [
                    in_ref[src, pl.ds(S_ROW + (seq * 2 + block) * 32, 32), :]
                    for src in range(4)
                ],
                axis=0,
            )
            carried.append(dot(readout[seq * 64 : seq * 64 + 64], state))
        factor = jnp.where(
            low, grow[:, 2 * block : 2 * block + 1], grow[:, 2 * block + 1 : 2 * block + 2]
        )
        lanes = pl.ds(block * 128, 128)
        y = y + jnp.concatenate(carried, axis=0) * factor + skip_ref[:, lanes] * x.astype(F32)
        gated = y * (z / (1.0 + jnp.exp(-z)))
        squares = squares + jnp.sum(gated * gated, axis=1, keepdims=True)
        parts.append((gated * gain_ref[:, lanes]).astype(BF16))
    act = jnp.concatenate(parts, axis=1)
    first = jnp.where(col == (row % 2) * 64 + row // 2, 1.0, 0.0).astype(BF16)
    other = (row // 8) * 8 + (row + 4) % 8
    second = jnp.where(col == (other % 2) * 64 + other // 2, 1.0, 0.0).astype(BF16)
    lhs_a = dot(first, act).astype(BF16)
    lhs_b = dot(second, act).astype(BF16)
    squares = jnp.broadcast_to(squares, (128, 128)).astype(BF16)

    def store(a, b, first, width):
        lanes = pl.ds(first, width)
        a = a.reshape(16, 8, width)
        b = b.reshape(16, 8, width)
        upper = iota((16, 8, width), 1) < 4
        even = jnp.where(upper, a, b)
        odd = jnp.where(upper, b, a)
        o_buf[:, :, lanes] = jnp.stack([even, odd], axis=1).reshape(32, 8, width).astype(BF16)

    def leave(first, width, slot):
        lanes = pl.ds(first, width)
        copy = pltpu.make_async_copy(
            o_buf.at[:, :, lanes], out_ref.at[:, :, lanes], out_sems.at[slot]
        )
        copy.start()
        return copy

    store(dot(first, squares), dot(second, squares), HALF, 128)
    leaving = [leave(HALF, 128, 4)]
    fetch.wait()
    for chunk in range(8):
        lanes = pl.ds(chunk * 256, 256)
        a = dot(lhs_a, w_buf[:, lanes])
        b = dot(lhs_b, w_buf[:, pl.ds(HALF + chunk * 256, 256)])
        store(a, b, chunk * 256, 256)
        if chunk % 2:
            leaving.append(leave((chunk - 1) * 256, 512, chunk // 2))
    for copy in leaving:
        copy.wait()


def attend_kernel(
    where_ref,
    len_ref,
    acc_ref,
    in_ref,
    run_ref,
    rate_ref,
    k_ref,
    v_ref,
    dk_ref,
    dv_ref,
    near_ref,
    next_ref,
    across_ref,
    last_ref,
    out_ref,
):
    tok = where_ref[0]
    scale = 128 ** (-0.5)
    cache = k_ref.shape[1]
    for seq in range(2):
        queries = jnp.concatenate(
            [in_ref[src, pl.ds(Q_ROW + seq * 64, 64), :] for src in range(4)], axis=0
        )
        old = dot_t(queries, k_ref[seq]) * scale
        new = dot_t(queries, dk_ref[seq]) * scale
        limit = len_ref[seq] - tok * cache
        old = jnp.where(iota(old.shape, 1) < limit, old, MASKED)
        line = iota(new.shape, 0)
        draft = (line // 64) * 16 + line % 16
        new = jnp.where(iota(new.shape, 1) + tok * 16 <= draft, new, MASKED)
        peak = jnp.maximum(
            jnp.max(old, axis=1, keepdims=True), jnp.max(new, axis=1, keepdims=True)
        )
        peak = jnp.maximum(peak, FLOOR).astype(BF16).astype(F32)
        old = jnp.exp(old - peak)
        new = jnp.exp(new - peak)
        total = jnp.sum(old, axis=1, keepdims=True) + jnp.sum(new, axis=1, keepdims=True)
        numer = dot(old.astype(BF16), v_ref[seq]) + dot(new.astype(BF16), dv_ref[seq])
        numer = numer.astype(BF16)
        stats = jnp.where(iota((256, 128), 1) < 64, peak, total).astype(BF16)
        for to in range(4):
            out_ref[to, pl.ds(N_ROW + seq * 64, 64), :] = numer[to * 64 : to * 64 + 64]
            out_ref[to, pl.ds(M_ROW + seq * 64, 64), :] = stats[to * 64 : to * 64 + 64]

    row = iota((128, 128), 0)
    low = iota((128, 128), 1) < 64
    low_row = iota((1, 128), 1) < 64
    steps = all_steps(in_ref)
    inflow_t = both(in_ref, B_ROW, 16).astype(F32).T.astype(BF16)
    run = run_ref[...]
    rate = rate_ref[...]
    for seq in range(2):
        alive = (row >= seq * 64) & (row < seq * 64 + acc_ref[seq])
        end = -jnp.sum(jnp.where(alive, steps, 0.0), axis=0, keepdims=True) * rate
        weights = jnp.where(alive, jnp.exp(jnp.where(alive, end - run, 0.0)) * steps, 0.0)
        keep = jnp.exp(end)
        for block in range(2):
            first, second = 2 * block, 2 * block + 1
            x = both(in_ref, X_ROW + block * 16, 32).astype(F32)
            factor = jnp.where(
                low, weights[:, first : first + 1], weights[:, second : second + 1]
            )
            added = dot(inflow_t, (x * factor).astype(BF16))
            decay = jnp.where(low_row, keep[:, first : first + 1], keep[:, second : second + 1])
            for src in range(4):
                at = (seq * 2 + block) * 32
                state = in_ref[src, pl.ds(S_ROW + at, 32), :].astype(F32)
                result = decay * state + added[src * 32 : src * 32 + 32]
                out_ref[src, pl.ds(H_ROW + at, 32), :] = result.astype(BF16)
    for shift, ref in enumerate((near_ref, next_ref, across_ref, last_ref)):
        ref[...] = out_ref[lax.rem(tok + shift, 4)]


def combine_kernel(where_ref, near_ref, next_ref, across_ref, last_ref, att_ref, state_ref):
    refs = (near_ref, next_ref, across_ref, last_ref)
    for seq in range(2):
        stats = [ref[pl.ds(M_ROW + seq * 64, 64), :].astype(F32) for ref in refs]
        peaks = [s[:, 0:1] for s in stats]
        overall = functools.reduce(jnp.maximum, peaks)
        numer = jnp.zeros((64, 128), F32)
        denominator = jnp.zeros((64, 1), F32)
        for ref, peak, stat in zip(refs, peaks, stats):
            rescale = jnp.exp(peak - overall)
            denominator = denominator + rescale * stat[:, 64:65]
            part = ref[pl.ds(N_ROW + seq * 64, 64), :].astype(F32)
            numer = numer + rescale * part
        context = (numer / denominator).astype(BF16)
        for head in range(4):
            att_ref[seq, :, pl.ds(head * 128, 128)] = context[head * 16 : head * 16 + 16]
        for shift, ref in enumerate(refs):
            src = lax.rem(where_ref[0] + 4 - shift, 4)
            for block in range(2):
                pair = ref[pl.ds(H_ROW + (seq * 2 + block) * 32, 32), :]
                state_ref[seq, src * 4 + block * 2] = pair[:, :64]
                state_ref[seq, src * 4 + block * 2 + 1] = pair[:, 64:]


def sum_kernel(in_ref, out_ref):
    squares = in_ref[:, :, pl.ds(HALF, 128)].astype(F32)
    squares = squares.reshape(8, 4, 8, 128).sum(axis=1)
    scale = lax.rsqrt(squares * (1.0 / 1024.0) + EPSILON)
    swapped = lax.axis_index("tok") % 2 == 1
    for chunk in range(HALF // 128):
        part = in_ref[:, :, pl.ds(chunk * 128, 128)].astype(F32)
        part = part.reshape(8, 4, 8, 128).sum(axis=1)
        total = (part * scale).sum(axis=0)
        flipped = jnp.concatenate([total[4:8], total[0:4]], axis=0)
        total = jnp.where(swapped, flipped, total).astype(BF16)
        for draft in range(2):
            for half in range(2):
                rows = total[half * 4 + draft * 2 : half * 4 + draft * 2 + 2]
                out_ref[draft, :, pl.ds(half * HALF + chunk * 128, 128)] = rows


def in_vmem(count):
    return [pl.BlockSpec(memory_space=pltpu.VMEM) for _ in range(count)]


def in_smem(count):
    return [pl.BlockSpec(memory_space=pltpu.SMEM) for _ in range(count)]


def held(array):
    if INTERPRET:
        return array
    return pltpu.with_memory_space_constraint(array, pltpu.VMEM)


def call(kernel, ins, outs, cost, out_specs=None, **kwargs):
    flops, moved = cost
    return pl.pallas_call(
        kernel,
        in_specs=ins,
        out_specs=tuple(in_vmem(len(outs))) if out_specs is None else out_specs,
        out_shape=tuple(
            (jax.ShapeDtypeStruct if plain else pltpu.VMEM)(s, d) for s, d, plain in outs
        ),
        cost_estimate=pl.CostEstimate(flops=flops, bytes_accessed=moved, transcendentals=0),
        interpret=INTERPRET,
        **kwargs,
    )


def body(
    mamba_input,
    gate_input,
    in_b,
    in_c,
    step_size,
    decay_rate,
    skip_weight,
    norm_gain,
    ssm_state,
    out_weight,
    queries,
    draft_token_keys,
    draft_values,
    cached_key_rows,
    cache_values,
    cache_len,
    accepted,
):
    tok = lax.axis_index("tok")
    where = tok.reshape(1).astype(jnp.int32)
    (packed,) = call(
        pack_kernel,
        in_vmem(7),
        [((4, ROWS, 128), BF16, True)],
        (0, 1500000),
        out_specs=(pl.BlockSpec(memory_space=pl.ANY),),
        scratch_shapes=[pltpu.VMEM((4, ROWS, 128), BF16), pltpu.SemaphoreType.DMA((4,))],
    )(
        mamba_input,
        gate_input,
        in_b,
        in_c,
        step_size,
        jnp.swapaxes(ssm_state, 2, 3),
        queries,
    )
    arrived = lax.all_to_all(packed, "tok", split_axis=0, concat_axis=0, tiled=True)
    arrived = held(arrived)
    rate = jnp.pad(lax.dynamic_slice(decay_rate, (tok * 4,), (4,)), (0, 124)).reshape(1, 128)
    skip = jnp.repeat(lax.dynamic_slice(skip_weight, (tok * 4,), (4,)), 64).reshape(1, 256)
    gain = lax.dynamic_slice(norm_gain, (tok * 256,), (256,)).reshape(1, 256)
    shares, run = call(
        mixer_kernel,
        in_vmem(1) + [pl.BlockSpec(memory_space=pl.ANY)] + in_vmem(3),
        [((32, 8, WIDTH), BF16, True), ((128, 128), F32, INTERPRET)],
        (400000000, 4000000),
        out_specs=(pl.BlockSpec(memory_space=pl.ANY), *in_vmem(1)),
        scratch_shapes=[
            pltpu.VMEM((256, 4096), BF16),
            pltpu.VMEM((32, 8, WIDTH), BF16),
            pltpu.SemaphoreType.DMA,
            pltpu.SemaphoreType.DMA((5,)),
        ],
    )(arrived, out_weight, held(rate), held(skip), held(gain))
    landed = lax.all_to_all(shares, ("head", "tok"), split_axis=0, concat_axis=0, tiled=True)
    back = call(
        attend_kernel,
        in_smem(3) + in_vmem(7),
        [((BACK_ROWS, 128), BF16, INTERPRET)] * 4,
        (0, 0),
        scratch_shapes=[pltpu.VMEM((4, BACK_ROWS, 128), BF16)],
    )(
        where,
        cache_len,
        accepted,
        arrived,
        held(run),
        held(rate),
        cached_key_rows,
        cache_values,
        draft_token_keys,
        draft_values,
    )
    returned = [held(back[0])] + [
        held(lax.ppermute(back[k], "tok", [(i, (i + k) % 4) for i in range(4)]))
        for k in (1, 2, 3)
    ]
    attn_context, state_t = call(
        combine_kernel,
        in_smem(1) + in_vmem(4),
        [((2, 16, 512), BF16, True), ((2, 16, 32, 64), BF16, True)],
        (0, 0),
    )(where, *returned)
    (mamba_out,) = call(
        sum_kernel, in_vmem(1), [((2, 2, 4096), BF16, True)], (1000000, 1500000)
    )(held(landed))
    return (mamba_out, attn_context, jnp.swapaxes(state_t, 2, 3))


def solution(mesh):
    in_specs = (
        P("dp", "tok", "head"),
        P("dp", "tok", "head"),
        P("dp", "tok", "head"),
        P("dp", "tok", "head"),
        P("dp", "tok", "head"),
        P("head"),
        P("head"),
        P("head"),
        P("dp", "head", None, "tok"),
        P(("head", "tok"), None),
        P("dp", "tok", "head"),
        P("dp", "tok", "head"),
        P("dp", "tok", "head"),
        P("dp", "tok", "head"),
        P("dp", "tok", "head"),
        P("dp"),
        P("dp"),
    )
    out_specs = (
        P(("head", "tok"), "dp", None),
        P("dp", "tok", "head"),
        P("dp", "head", None, "tok"),
    )
    return jax.shard_map(body, mesh=mesh, in_specs=in_specs, out_specs=out_specs, check_vma=False)
```

```python
import functools

import jax
import jax.numpy as jnp
from jax import lax
from jax.experimental import pallas as pl
from jax.experimental.pallas import tpu as pltpu
from jax.sharding import PartitionSpec as P

EPSILON = 1e-05
MASKED = -1e30
FLOOR = -1e20
INTERPRET = False

F32 = jnp.float32
BF16 = jnp.bfloat16

X_ROW = 0
Z_ROW = 64
B_ROW = 128
C_ROW = 160
S_ROW = 192
T_ROW = 320
ROWS = 336

N_ROW = 0
M_ROW = 128
H_ROW = 256
BACK_ROWS = 384

HALF = 2048
WIDTH = HALF + 128


def dot(a, b):
    return jnp.dot(a, b, preferred_element_type=F32)


def dot_t(a, b):
    return lax.dot_general(a, b, (((1,), (1,)), ((), ())), preferred_element_type=F32)


def iota(shape, dim):
    return lax.broadcasted_iota(jnp.int32, shape, dim)


def pack_kernel(x_ref, z_ref, b_ref, c_ref, t_ref, s_ref, q_ref, out_ref, mine_ref, buf, sems):
    pad = jnp.zeros((16, 60), F32)
    copies = []
    for to in range(4):
        for seq in range(2):
            for block in range(2):
                lanes = pl.ds(to * 256 + block * 128, 128)
                row = (seq * 2 + block) * 16
                buf[to, pl.ds(X_ROW + row, 16), :] = x_ref[seq, :, lanes]
                buf[to, pl.ds(Z_ROW + row, 16), :] = z_ref[seq, :, lanes]
                head = to * 4 + block * 2
                pair = jnp.concatenate([s_ref[seq, head], s_ref[seq, head + 1]], axis=1)
                buf[to, pl.ds(S_ROW + (seq * 2 + block) * 32, 32), :] = pair
            buf[to, pl.ds(B_ROW + seq * 16, 16), :] = b_ref[seq]
            buf[to, pl.ds(C_ROW + seq * 16, 16), :] = c_ref[seq]
        own = [t_ref[seq].astype(F32)[:, to * 4 : to * 4 + 4] for seq in range(2)]
        lanes = jnp.concatenate([own[0], pad, own[1], pad], axis=1)
        buf[to, pl.ds(T_ROW, 16), :] = lanes.astype(BF16)
        copy = pltpu.make_async_copy(buf.at[to], out_ref.at[to], sems.at[to])
        copy.start()
        copies.append(copy)
    for seq in range(2):
        for head in range(4):
            row = (seq * 4 + head) * 16
            mine_ref[pl.ds(row, 16), :] = q_ref[seq, :, pl.ds(head * 128, 128)]
    for copy in copies:
        copy.wait()


def all_steps(in_ref):
    both_lanes = jnp.concatenate(
        [in_ref[src, pl.ds(T_ROW, 16), :].astype(F32) for src in range(4)], axis=0
    )
    swapped = jnp.concatenate([both_lanes[:, 64:], both_lanes[:, :64]], axis=1)
    return jnp.concatenate([both_lanes, swapped], axis=0)


def both(in_ref, first, stride):
    return jnp.concatenate(
        [in_ref[src, pl.ds(first + seq * stride, 16), :] for seq in range(2) for src in range(4)],
        axis=0,
    )


def mixer_kernel(
    in_ref,
    w_ref,
    rate_ref,
    skip_ref,
    gain_ref,
    mine_ref,
    before_ref,
    out_ref,
    run_ref,
    pair_ref,
    w_buf,
    o_buf,
    sem,
    out_sems,
):
    pair_ref[0] = mine_ref[...]
    pair_ref[1] = before_ref[...]
    fetch = pltpu.make_async_copy(w_ref, w_buf, sem)
    fetch.start()
    row = iota((128, 128), 0)
    col = iota((128, 128), 1)
    low = col < 64
    causal = (row >= col) & ((row >= 64) == (col >= 64))
    ones = jnp.where(causal, 1.0, 0.0).astype(BF16)
    steps = all_steps(in_ref)
    total = dot(ones, steps.astype(BF16))
    rate = rate_ref[...]
    run = -total * rate
    run_ref[...] = run
    run_t = run.T
    steps_t = steps.T
    grow = jnp.exp(run)
    inflow = both(in_ref, B_ROW, 16)
    readout = both(in_ref, C_ROW, 16)
    affinity = dot_t(readout, inflow)
    squares = jnp.zeros((128, 1), F32)
    parts = []
    for block in range(2):
        x = both(in_ref, X_ROW + block * 16, 32)
        z = both(in_ref, Z_ROW + block * 16, 32).astype(F32)
        mixed = []
        for half in range(2):
            head = block * 2 + half
            gap = jnp.where(causal, run[:, head : head + 1] - run_t[head : head + 1, :], 0.0)
            mixing = jnp.where(
                causal, jnp.exp(gap) * steps_t[head : head + 1, :] * affinity, 0.0
            )
            mixed.append(dot(mixing.astype(BF16), x))
        y = jnp.where(low, mixed[0], mixed[1])
        carried = []
        for seq in range(2):
            state = jnp.concatenate(
                [
                    in_ref[src, pl.ds(S_ROW + (seq * 2 + block) * 32, 32), :]
                    for src in range(4)
                ],
                axis=0,
            )
            carried.append(dot(readout[seq * 64 : seq * 64 + 64], state))
        factor = jnp.where(
            low, grow[:, 2 * block : 2 * block + 1], grow[:, 2 * block + 1 : 2 * block + 2]
        )
        lanes = pl.ds(block * 128, 128)
        y = y + jnp.concatenate(carried, axis=0) * factor + skip_ref[:, lanes] * x.astype(F32)
        gated = y * (z / (1.0 + jnp.exp(-z)))
        squares = squares + jnp.sum(gated * gated, axis=1, keepdims=True)
        parts.append((gated * gain_ref[:, lanes]).astype(BF16))
    act = jnp.concatenate(parts, axis=1)
    first = jnp.where(col == (row % 2) * 64 + row // 2, 1.0, 0.0).astype(BF16)
    other = (row // 8) * 8 + (row + 4) % 8
    second = jnp.where(col == (other % 2) * 64 + other // 2, 1.0, 0.0).astype(BF16)
    lhs_a = dot(first, act).astype(BF16)
    lhs_b = dot(second, act).astype(BF16)
    squares = jnp.broadcast_to(squares, (128, 128)).astype(BF16)

    def store(a, b, first, width):
        lanes = pl.ds(first, width)
        a = a.reshape(16, 8, width)
        b = b.reshape(16, 8, width)
        upper = iota((16, 8, width), 1) < 4
        even = jnp.where(upper, a, b)
        odd = jnp.where(upper, b, a)
        o_buf[:, :, lanes] = jnp.stack([even, odd], axis=1).reshape(32, 8, width).astype(BF16)

    def leave(first, width, slot):
        lanes = pl.ds(first, width)
        copy = pltpu.make_async_copy(
            o_buf.at[:, :, lanes], out_ref.at[:, :, lanes], out_sems.at[slot]
        )
        copy.start()
        return copy

    store(dot(first, squares), dot(second, squares), HALF, 128)
    leaving = [leave(HALF, 128, 4)]
    fetch.wait()
    for chunk in range(8):
        lanes = pl.ds(chunk * 256, 256)
        a = dot(lhs_a, w_buf[:, lanes])
        b = dot(lhs_b, w_buf[:, pl.ds(HALF + chunk * 256, 256)])
        store(a, b, chunk * 256, 256)
        if chunk % 2:
            leaving.append(leave((chunk - 1) * 256, 512, chunk // 2))
    for copy in leaving:
        copy.wait()


def attend(tok, seq, queries, backs, limit, k_ref, v_ref, dk_ref, dv_ref, refs):
    scale = 128 ** (-0.5)
    old = dot_t(queries, k_ref[seq]) * scale
    new = dot_t(queries, dk_ref[seq]) * scale
    old = jnp.where(iota(old.shape, 1) < limit, old, MASKED)
    line = iota(new.shape, 0)
    draft = ((tok + 4 - backs[0] - line // 64) % 4) * 16 + line % 16
    new = jnp.where(iota(new.shape, 1) + tok * 16 <= draft, new, MASKED)
    peak = jnp.maximum(jnp.max(old, axis=1, keepdims=True), jnp.max(new, axis=1, keepdims=True))
    peak = jnp.maximum(peak, FLOOR).astype(BF16).astype(F32)
    old = jnp.exp(old - peak)
    new = jnp.exp(new - peak)
    total = jnp.sum(old, axis=1, keepdims=True) + jnp.sum(new, axis=1, keepdims=True)
    numer = dot(old.astype(BF16), v_ref[seq]) + dot(new.astype(BF16), dv_ref[seq])
    numer = numer.astype(BF16)
    stats = jnp.where(iota((128, 128), 1) < 64, peak, total).astype(BF16)
    for part, ref in enumerate(refs):
        ref[pl.ds(N_ROW + seq * 64, 64), :] = numer[part * 64 : part * 64 + 64]
        ref[pl.ds(M_ROW + seq * 64, 64), :] = stats[part * 64 : part * 64 + 64]


def near_kernel(
    where_ref,
    len_ref,
    acc_ref,
    in_ref,
    pair_ref,
    run_ref,
    rate_ref,
    k_ref,
    v_ref,
    dk_ref,
    dv_ref,
    near_ref,
    last_ref,
    state_ref,
    out_ref,
):
    tok = where_ref[0]
    row = iota((128, 128), 0)
    low = iota((128, 128), 1) < 64
    low_row = iota((1, 128), 1) < 64
    steps = all_steps(in_ref)
    inflow_t = both(in_ref, B_ROW, 16).astype(F32).T.astype(BF16)
    run = run_ref[...]
    rate = rate_ref[...]
    for seq in range(2):
        rows = pl.ds(seq * 64, 64)
        queries = jnp.concatenate([pair_ref[0, rows], pair_ref[1, rows]], axis=0)
        limit = len_ref[seq] - tok * k_ref.shape[1]
        attend(
            tok, seq, queries, (0, 1), limit, k_ref, v_ref, dk_ref, dv_ref, (near_ref, last_ref)
        )
        alive = (row >= seq * 64) & (row < seq * 64 + acc_ref[seq])
        end = -jnp.sum(jnp.where(alive, steps, 0.0), axis=0, keepdims=True) * rate
        weights = jnp.where(alive, jnp.exp(jnp.where(alive, end - run, 0.0)) * steps, 0.0)
        keep = jnp.exp(end)
        for block in range(2):
            first, second = 2 * block, 2 * block + 1
            x = both(in_ref, X_ROW + block * 16, 32).astype(F32)
            factor = jnp.where(
                low, weights[:, first : first + 1], weights[:, second : second + 1]
            )
            added = dot(inflow_t, (x * factor).astype(BF16))
            decay = jnp.where(low_row, keep[:, first : first + 1], keep[:, second : second + 1])
            for src in range(4):
                at = (seq * 2 + block) * 32
                state = in_ref[src, pl.ds(S_ROW + at, 32), :].astype(F32)
                result = decay * state + added[src * 32 : src * 32 + 32]
                out_ref[src, pl.ds(at, 32), :] = result.astype(BF16)
    near_ref[pl.ds(H_ROW, 128), :] = out_ref[tok]
    last_ref[pl.ds(H_ROW, 128), :] = out_ref[lax.rem(tok + 3, 4)]
    for shift in (1, 2):
        state_ref[shift - 1] = out_ref[lax.rem(tok + shift, 4)]


def far_kernel(
    where_ref,
    len_ref,
    farther_ref,
    state_ref,
    k_ref,
    v_ref,
    dk_ref,
    dv_ref,
    next_ref,
    across_ref,
):
    tok = where_ref[0]
    for seq in range(2):
        rows = pl.ds(seq * 64, 64)
        queries = jnp.concatenate([farther_ref[0, rows], farther_ref[1, rows]], axis=0)
        limit = len_ref[seq] - tok * k_ref.shape[1]
        attend(
            tok, seq, queries, (2, 3), limit, k_ref, v_ref, dk_ref, dv_ref, (across_ref, next_ref)
        )
    next_ref[pl.ds(H_ROW, 128), :] = state_ref[0]
    across_ref[pl.ds(H_ROW, 128), :] = state_ref[1]


def combine_kernel(where_ref, near_ref, next_ref, across_ref, last_ref, att_ref, state_ref):
    refs = (near_ref, next_ref, across_ref, last_ref)
    for seq in range(2):
        stats = [ref[pl.ds(M_ROW + seq * 64, 64), :].astype(F32) for ref in refs]
        peaks = [s[:, 0:1] for s in stats]
        overall = functools.reduce(jnp.maximum, peaks)
        numer = jnp.zeros((64, 128), F32)
        denominator = jnp.zeros((64, 1), F32)
        for ref, peak, stat in zip(refs, peaks, stats):
            rescale = jnp.exp(peak - overall)
            denominator = denominator + rescale * stat[:, 64:65]
            part = ref[pl.ds(N_ROW + seq * 64, 64), :].astype(F32)
            numer = numer + rescale * part
        context = (numer / denominator).astype(BF16)
        for head in range(4):
            att_ref[seq, :, pl.ds(head * 128, 128)] = context[head * 16 : head * 16 + 16]
        for shift, ref in enumerate(refs):
            src = lax.rem(where_ref[0] + 4 - shift, 4)
            for block in range(2):
                pair = ref[pl.ds(H_ROW + (seq * 2 + block) * 32, 32), :]
                state_ref[seq, src * 4 + block * 2] = pair[:, :64]
                state_ref[seq, src * 4 + block * 2 + 1] = pair[:, 64:]


def sum_kernel(in_ref, out_ref):
    squares = in_ref[:, :, pl.ds(HALF, 128)].astype(F32)
    squares = squares.reshape(8, 4, 8, 128).sum(axis=1)
    scale = lax.rsqrt(squares * (1.0 / 1024.0) + EPSILON)
    swapped = lax.axis_index("tok") % 2 == 1
    for chunk in range(HALF // 128):
        part = in_ref[:, :, pl.ds(chunk * 128, 128)].astype(F32)
        part = part.reshape(8, 4, 8, 128).sum(axis=1)
        total = (part * scale).sum(axis=0)
        flipped = jnp.concatenate([total[4:8], total[0:4]], axis=0)
        total = jnp.where(swapped, flipped, total).astype(BF16)
        for draft in range(2):
            for half in range(2):
                rows = total[half * 4 + draft * 2 : half * 4 + draft * 2 + 2]
                out_ref[draft, :, pl.ds(half * HALF + chunk * 128, 128)] = rows


def in_vmem(count):
    return [pl.BlockSpec(memory_space=pltpu.VMEM) for _ in range(count)]


def in_smem(count):
    return [pl.BlockSpec(memory_space=pltpu.SMEM) for _ in range(count)]


def held(array):
    if INTERPRET:
        return array
    return pltpu.with_memory_space_constraint(array, pltpu.VMEM)


def call(kernel, ins, outs, cost, out_specs=None, **kwargs):
    flops, moved = cost
    return pl.pallas_call(
        kernel,
        in_specs=ins,
        out_specs=tuple(in_vmem(len(outs))) if out_specs is None else out_specs,
        out_shape=tuple(
            (jax.ShapeDtypeStruct if plain else pltpu.VMEM)(s, d) for s, d, plain in outs
        ),
        cost_estimate=pl.CostEstimate(flops=flops, bytes_accessed=moved, transcendentals=0),
        interpret=INTERPRET,
        **kwargs,
    )


def body(
    mamba_input,
    gate_input,
    in_b,
    in_c,
    step_size,
    decay_rate,
    skip_weight,
    norm_gain,
    ssm_state,
    out_weight,
    queries,
    draft_token_keys,
    draft_values,
    cached_key_rows,
    cache_values,
    cache_len,
    accepted,
):
    tok = lax.axis_index("tok")
    where = tok.reshape(1).astype(jnp.int32)
    packed, mine = call(
        pack_kernel,
        in_vmem(7),
        [((4, ROWS, 128), BF16, True), ((128, 128), BF16, INTERPRET)],
        (0, 1500000),
        out_specs=(pl.BlockSpec(memory_space=pl.ANY), *in_vmem(1)),
        scratch_shapes=[pltpu.VMEM((4, ROWS, 128), BF16), pltpu.SemaphoreType.DMA((4,))],
    )(
        mamba_input,
        gate_input,
        in_b,
        in_c,
        step_size,
        jnp.swapaxes(ssm_state, 2, 3),
        queries,
    )
    arrived = lax.all_to_all(packed, "tok", split_axis=0, concat_axis=0, tiled=True)
    arrived = held(arrived)
    before = lax.ppermute(mine, "tok", [(i, (i + 1) % 4) for i in range(4)])
    rate = jnp.pad(lax.dynamic_slice(decay_rate, (tok * 4,), (4,)), (0, 124)).reshape(1, 128)
    skip = jnp.repeat(lax.dynamic_slice(skip_weight, (tok * 4,), (4,)), 64).reshape(1, 256)
    gain = lax.dynamic_slice(norm_gain, (tok * 256,), (256,)).reshape(1, 256)
    shares, run, pair = call(
        mixer_kernel,
        in_vmem(1) + [pl.BlockSpec(memory_space=pl.ANY)] + in_vmem(5),
        [
            ((32, 8, WIDTH), BF16, True),
            ((128, 128), F32, INTERPRET),
            ((2, 128, 128), BF16, INTERPRET),
        ],
        (400000000, 4000000),
        out_specs=(pl.BlockSpec(memory_space=pl.ANY), *in_vmem(2)),
        scratch_shapes=[
            pltpu.VMEM((256, 4096), BF16),
            pltpu.VMEM((32, 8, WIDTH), BF16),
            pltpu.SemaphoreType.DMA,
            pltpu.SemaphoreType.DMA((5,)),
        ],
    )(arrived, out_weight, held(rate), held(skip), held(gain), held(mine), held(before))
    farther = lax.ppermute(pair, "tok", [(i, (i + 2) % 4) for i in range(4)])
    landed = lax.all_to_all(shares, ("head", "tok"), split_axis=0, concat_axis=0, tiled=True)
    cached = (cached_key_rows, cache_values, draft_token_keys, draft_values)
    back = ((BACK_ROWS, 128), BF16, INTERPRET)
    near, last, states = call(
        near_kernel,
        in_smem(3) + in_vmem(8),
        [back, back, ((2, 128, 128), BF16, INTERPRET)],
        (0, 0),
        scratch_shapes=[pltpu.VMEM((4, 128, 128), BF16)],
    )(where, cache_len, accepted, arrived, held(pair), held(run), held(rate), *cached)
    after, across = call(far_kernel, in_smem(2) + in_vmem(6), [back, back], (0, 0))(
        where, cache_len, held(farther), held(states), *cached
    )
    returned = [held(near)] + [
        held(lax.ppermute(part, "tok", [(i, (i + shift) % 4) for i in range(4)]))
        for shift, part in ((1, after), (2, across), (3, last))
    ]
    attn_context, state_t = call(
        combine_kernel,
        in_smem(1) + in_vmem(4),
        [((2, 16, 512), BF16, True), ((2, 16, 32, 64), BF16, True)],
        (0, 0),
    )(where, *returned)
    (mamba_out,) = call(
        sum_kernel, in_vmem(1), [((2, 2, 4096), BF16, True)], (1000000, 1500000)
    )(held(landed))
    return (mamba_out, attn_context, jnp.swapaxes(state_t, 2, 3))


def solution(mesh):
    in_specs = (
        P("dp", "tok", "head"),
        P("dp", "tok", "head"),
        P("dp", "tok", "head"),
        P("dp", "tok", "head"),
        P("dp", "tok", "head"),
        P("head"),
        P("head"),
        P("head"),
        P("dp", "head", None, "tok"),
        P(("head", "tok"), None),
        P("dp", "tok", "head"),
        P("dp", "tok", "head"),
        P("dp", "tok", "head"),
        P("dp", "tok", "head"),
        P("dp", "tok", "head"),
        P("dp"),
        P("dp"),
    )
    out_specs = (
        P(("head", "tok"), "dp", None),
        P("dp", "tok", "head"),
        P("dp", "head", None, "tok"),
    )
    return jax.shard_map(body, mesh=mesh, in_specs=in_specs, out_specs=out_specs, check_vma=False)
```

```python
import functools

import jax
import jax.numpy as jnp
from jax import lax
from jax.experimental import pallas as pl
from jax.experimental.pallas import tpu as pltpu
from jax.sharding import PartitionSpec as P

EPSILON = 1e-05
MASKED = -1e30
FLOOR = -1e20
INTERPRET = False

F32 = jnp.float32
BF16 = jnp.bfloat16

X_ROW = 0
Z_ROW = 64
B_ROW = 128
C_ROW = 160
S_ROW = 192
T_ROW = 320
ROWS = 336

N_ROW = 0
M_ROW = 128
H_ROW = 144
BACK_ROWS = 272

HALF = 2048
WIDTH = HALF + 128


def dot(a, b):
    return jnp.dot(a, b, preferred_element_type=F32)


def dot_t(a, b):
    return lax.dot_general(a, b, (((1,), (1,)), ((), ())), preferred_element_type=F32)


def iota(shape, dim):
    return lax.broadcasted_iota(jnp.int32, shape, dim)


def pack_kernel(x_ref, z_ref, b_ref, c_ref, t_ref, s_ref, q_ref, out_ref, mine_ref, buf, sems):
    pad = jnp.zeros((16, 60), F32)
    copies = []
    for to in range(4):
        for seq in range(2):
            for block in range(2):
                lanes = pl.ds(to * 256 + block * 128, 128)
                row = (seq * 2 + block) * 16
                buf[to, pl.ds(X_ROW + row, 16), :] = x_ref[seq, :, lanes]
                buf[to, pl.ds(Z_ROW + row, 16), :] = z_ref[seq, :, lanes]
                head = to * 4 + block * 2
                pair = jnp.concatenate([s_ref[seq, head], s_ref[seq, head + 1]], axis=1)
                buf[to, pl.ds(S_ROW + (seq * 2 + block) * 32, 32), :] = pair
            buf[to, pl.ds(B_ROW + seq * 16, 16), :] = b_ref[seq]
            buf[to, pl.ds(C_ROW + seq * 16, 16), :] = c_ref[seq]
        own = [t_ref[seq].astype(F32)[:, to * 4 : to * 4 + 4] for seq in range(2)]
        lanes = jnp.concatenate([own[0], pad, own[1], pad], axis=1)
        buf[to, pl.ds(T_ROW, 16), :] = lanes.astype(BF16)
        copy = pltpu.make_async_copy(buf.at[to], out_ref.at[to], sems.at[to])
        copy.start()
        copies.append(copy)
    for seq in range(2):
        for head in range(4):
            row = (seq * 4 + head) * 16
            mine_ref[pl.ds(row, 16), :] = q_ref[seq, :, pl.ds(head * 128, 128)]
    for copy in copies:
        copy.wait()


def all_steps(in_ref):
    both_lanes = jnp.concatenate(
        [in_ref[src, pl.ds(T_ROW, 16), :].astype(F32) for src in range(4)], axis=0
    )
    swapped = jnp.concatenate([both_lanes[:, 64:], both_lanes[:, :64]], axis=1)
    return jnp.concatenate([both_lanes, swapped], axis=0)


def both(in_ref, first, stride):
    return jnp.concatenate(
        [in_ref[src, pl.ds(first + seq * stride, 16), :] for seq in range(2) for src in range(4)],
        axis=0,
    )


def mixer_kernel(
    in_ref,
    w_ref,
    rate_ref,
    skip_ref,
    gain_ref,
    mine_ref,
    before_ref,
    out_ref,
    run_ref,
    pair_ref,
    w_buf,
    o_buf,
    sem,
    out_sems,
):
    pair_ref[0] = mine_ref[...]
    pair_ref[1] = before_ref[...]
    fetch = pltpu.make_async_copy(w_ref, w_buf, sem)
    fetch.start()
    row = iota((128, 128), 0)
    col = iota((128, 128), 1)
    low = col < 64
    causal = (row >= col) & ((row >= 64) == (col >= 64))
    ones = jnp.where(causal, 1.0, 0.0).astype(BF16)
    steps = all_steps(in_ref)
    total = dot(ones, steps.astype(BF16))
    rate = rate_ref[...]
    run = -total * rate
    run_ref[...] = run
    run_t = run.T
    steps_t = steps.T
    grow = jnp.exp(run)
    inflow = both(in_ref, B_ROW, 16)
    readout = both(in_ref, C_ROW, 16)
    affinity = dot_t(readout, inflow)
    squares = jnp.zeros((128, 1), F32)
    parts = []
    for block in range(2):
        x = both(in_ref, X_ROW + block * 16, 32)
        z = both(in_ref, Z_ROW + block * 16, 32).astype(F32)
        mixed = []
        for half in range(2):
            head = block * 2 + half
            gap = jnp.where(causal, run[:, head : head + 1] - run_t[head : head + 1, :], 0.0)
            mixing = jnp.where(
                causal, jnp.exp(gap) * steps_t[head : head + 1, :] * affinity, 0.0
            )
            mixed.append(dot(mixing.astype(BF16), x))
        y = jnp.where(low, mixed[0], mixed[1])
        carried = []
        for seq in range(2):
            state = jnp.concatenate(
                [
                    in_ref[src, pl.ds(S_ROW + (seq * 2 + block) * 32, 32), :]
                    for src in range(4)
                ],
                axis=0,
            )
            carried.append(dot(readout[seq * 64 : seq * 64 + 64], state))
        factor = jnp.where(
            low, grow[:, 2 * block : 2 * block + 1], grow[:, 2 * block + 1 : 2 * block + 2]
        )
        lanes = pl.ds(block * 128, 128)
        y = y + jnp.concatenate(carried, axis=0) * factor + skip_ref[:, lanes] * x.astype(F32)
        gated = y * (z / (1.0 + jnp.exp(-z)))
        squares = squares + jnp.sum(gated * gated, axis=1, keepdims=True)
        parts.append((gated * gain_ref[:, lanes]).astype(BF16))
    act = jnp.concatenate(parts, axis=1)
    first = jnp.where(col == (row % 2) * 64 + row // 2, 1.0, 0.0).astype(BF16)
    other = (row // 8) * 8 + (row + 4) % 8
    second = jnp.where(col == (other % 2) * 64 + other // 2, 1.0, 0.0).astype(BF16)
    lhs_a = dot(first, act).astype(BF16)
    lhs_b = dot(second, act).astype(BF16)
    squares = jnp.broadcast_to(squares, (128, 128)).astype(BF16)

    def store(a, b, first, width):
        lanes = pl.ds(first, width)
        a = a.reshape(16, 8, width)
        b = b.reshape(16, 8, width)
        upper = iota((16, 8, width), 1) < 4
        even = jnp.where(upper, a, b)
        odd = jnp.where(upper, b, a)
        o_buf[:, :, lanes] = jnp.stack([even, odd], axis=1).reshape(32, 8, width).astype(BF16)

    def leave(first, width, slot):
        lanes = pl.ds(first, width)
        copy = pltpu.make_async_copy(
            o_buf.at[:, :, lanes], out_ref.at[:, :, lanes], out_sems.at[slot]
        )
        copy.start()
        return copy

    store(dot(first, squares), dot(second, squares), HALF, 128)
    leaving = [leave(HALF, 128, 4)]
    fetch.wait()
    for chunk in range(8):
        lanes = pl.ds(chunk * 256, 256)
        a = dot(lhs_a, w_buf[:, lanes])
        b = dot(lhs_b, w_buf[:, pl.ds(HALF + chunk * 256, 256)])
        store(a, b, chunk * 256, 256)
        if chunk % 2:
            leaving.append(leave((chunk - 1) * 256, 512, chunk // 2))
    for copy in leaving:
        copy.wait()


def attend(tok, seq, queries, backs, limit, k_ref, v_ref, dk_ref, dv_ref, refs):
    scale = 128 ** (-0.5)
    old = dot_t(queries, k_ref[seq]) * scale
    new = dot_t(queries, dk_ref[seq]) * scale
    old = jnp.where(iota(old.shape, 1) < limit, old, MASKED)
    line = iota(new.shape, 0)
    draft = ((tok + 4 - backs[0] - line // 64) % 4) * 16 + line % 16
    new = jnp.where(iota(new.shape, 1) + tok * 16 <= draft, new, MASKED)
    peak = jnp.maximum(jnp.max(old, axis=1, keepdims=True), jnp.max(new, axis=1, keepdims=True))
    peak = jnp.maximum(peak, FLOOR).astype(BF16).astype(F32)
    old = jnp.exp(old - peak)
    new = jnp.exp(new - peak)
    total = jnp.sum(old, axis=1, keepdims=True) + jnp.sum(new, axis=1, keepdims=True)
    numer = dot(old.astype(BF16), v_ref[seq]) + dot(new.astype(BF16), dv_ref[seq])
    numer = numer.astype(BF16)
    lanes = iota((128, 128), 1)
    stats = jnp.where(lanes == 0, peak, total).T
    for part, ref in enumerate(refs):
        ref[pl.ds(N_ROW + seq * 64, 64), :] = numer[part * 64 : part * 64 + 64]
        own = stats[:8] if part == 0 else jnp.concatenate([stats[:8, 64:], stats[:8, :64]], axis=1)
        ref[pl.ds(M_ROW + seq * 8, 8), :] = own.astype(BF16)


def near_kernel(
    where_ref,
    len_ref,
    acc_ref,
    in_ref,
    pair_ref,
    run_ref,
    rate_ref,
    k_ref,
    v_ref,
    dk_ref,
    dv_ref,
    near_ref,
    last_ref,
    state_ref,
    out_ref,
):
    tok = where_ref[0]
    row = iota((128, 128), 0)
    low = iota((128, 128), 1) < 64
    low_row = iota((1, 128), 1) < 64
    steps = all_steps(in_ref)
    inflow_t = both(in_ref, B_ROW, 16).astype(F32).T.astype(BF16)
    run = run_ref[...]
    rate = rate_ref[...]
    for seq in range(2):
        rows = pl.ds(seq * 64, 64)
        queries = jnp.concatenate([pair_ref[0, rows], pair_ref[1, rows]], axis=0)
        limit = len_ref[seq] - tok * k_ref.shape[1]
        attend(
            tok, seq, queries, (0, 1), limit, k_ref, v_ref, dk_ref, dv_ref, (near_ref, last_ref)
        )
        alive = (row >= seq * 64) & (row < seq * 64 + acc_ref[seq])
        end = -jnp.sum(jnp.where(alive, steps, 0.0), axis=0, keepdims=True) * rate
        weights = jnp.where(alive, jnp.exp(jnp.where(alive, end - run, 0.0)) * steps, 0.0)
        keep = jnp.exp(end)
        for block in range(2):
            first, second = 2 * block, 2 * block + 1
            x = both(in_ref, X_ROW + block * 16, 32).astype(F32)
            factor = jnp.where(
                low, weights[:, first : first + 1], weights[:, second : second + 1]
            )
            added = dot(inflow_t, (x * factor).astype(BF16))
            decay = jnp.where(low_row, keep[:, first : first + 1], keep[:, second : second + 1])
            for src in range(4):
                at = (seq * 2 + block) * 32
                state = in_ref[src, pl.ds(S_ROW + at, 32), :].astype(F32)
                result = decay * state + added[src * 32 : src * 32 + 32]
                out_ref[src, pl.ds(at, 32), :] = result.astype(BF16)
    near_ref[pl.ds(H_ROW, 128), :] = out_ref[tok]
    last_ref[pl.ds(H_ROW, 128), :] = out_ref[lax.rem(tok + 3, 4)]
    for shift in (1, 2):
        state_ref[shift - 1] = out_ref[lax.rem(tok + shift, 4)]


def far_kernel(
    where_ref,
    len_ref,
    farther_ref,
    state_ref,
    k_ref,
    v_ref,
    dk_ref,
    dv_ref,
    next_ref,
    across_ref,
):
    tok = where_ref[0]
    for seq in range(2):
        rows = pl.ds(seq * 64, 64)
        queries = jnp.concatenate([farther_ref[0, rows], farther_ref[1, rows]], axis=0)
        limit = len_ref[seq] - tok * k_ref.shape[1]
        attend(
            tok, seq, queries, (2, 3), limit, k_ref, v_ref, dk_ref, dv_ref, (across_ref, next_ref)
        )
    next_ref[pl.ds(H_ROW, 128), :] = state_ref[0]
    across_ref[pl.ds(H_ROW, 128), :] = state_ref[1]


def combine_kernel(where_ref, near_ref, next_ref, across_ref, last_ref, att_ref, state_ref):
    refs = (near_ref, next_ref, across_ref, last_ref)
    for seq in range(2):
        stats = []
        for ref in refs:
            lines = ref[pl.ds(M_ROW + seq * 8, 8), :].astype(F32)
            stats.append(jnp.broadcast_to(lines[0:1], (128, 128)).T[:64])
            stats.append(jnp.broadcast_to(lines[1:2], (128, 128)).T[:64])
        peaks = stats[0::2]
        overall = functools.reduce(jnp.maximum, peaks)
        numer = jnp.zeros((64, 128), F32)
        denominator = jnp.zeros((64, 128), F32)
        for ref, peak, stat in zip(refs, peaks, stats[1::2]):
            rescale = jnp.exp(peak - overall)
            denominator = denominator + rescale * stat
            part = ref[pl.ds(N_ROW + seq * 64, 64), :].astype(F32)
            numer = numer + rescale * part
        context = (numer / denominator).astype(BF16)
        for head in range(4):
            att_ref[seq, :, pl.ds(head * 128, 128)] = context[head * 16 : head * 16 + 16]
        for shift, ref in enumerate(refs):
            src = lax.rem(where_ref[0] + 4 - shift, 4)
            for block in range(2):
                pair = ref[pl.ds(H_ROW + (seq * 2 + block) * 32, 32), :]
                state_ref[seq, src * 4 + block * 2] = pair[:, :64]
                state_ref[seq, src * 4 + block * 2 + 1] = pair[:, 64:]


def sum_kernel(in_ref, out_ref):
    squares = in_ref[:, :, pl.ds(HALF, 128)].astype(F32)
    squares = squares.reshape(8, 4, 8, 128).sum(axis=1)
    scale = lax.rsqrt(squares * (1.0 / 1024.0) + EPSILON)
    swapped = lax.axis_index("tok") % 2 == 1
    for chunk in range(HALF // 128):
        part = in_ref[:, :, pl.ds(chunk * 128, 128)].astype(F32)
        part = part.reshape(8, 4, 8, 128).sum(axis=1)
        total = (part * scale).sum(axis=0)
        flipped = jnp.concatenate([total[4:8], total[0:4]], axis=0)
        total = jnp.where(swapped, flipped, total).astype(BF16)
        for draft in range(2):
            for half in range(2):
                rows = total[half * 4 + draft * 2 : half * 4 + draft * 2 + 2]
                out_ref[draft, :, pl.ds(half * HALF + chunk * 128, 128)] = rows


def in_vmem(count):
    return [pl.BlockSpec(memory_space=pltpu.VMEM) for _ in range(count)]


def in_smem(count):
    return [pl.BlockSpec(memory_space=pltpu.SMEM) for _ in range(count)]


def held(array):
    if INTERPRET:
        return array
    return pltpu.with_memory_space_constraint(array, pltpu.VMEM)


def call(kernel, ins, outs, cost, out_specs=None, **kwargs):
    flops, moved = cost
    return pl.pallas_call(
        kernel,
        in_specs=ins,
        out_specs=tuple(in_vmem(len(outs))) if out_specs is None else out_specs,
        out_shape=tuple(
            (jax.ShapeDtypeStruct if plain else pltpu.VMEM)(s, d) for s, d, plain in outs
        ),
        cost_estimate=pl.CostEstimate(flops=flops, bytes_accessed=moved, transcendentals=0),
        interpret=INTERPRET,
        **kwargs,
    )


def body(
    mamba_input,
    gate_input,
    in_b,
    in_c,
    step_size,
    decay_rate,
    skip_weight,
    norm_gain,
    ssm_state,
    out_weight,
    queries,
    draft_token_keys,
    draft_values,
    cached_key_rows,
    cache_values,
    cache_len,
    accepted,
):
    tok = lax.axis_index("tok")
    where = tok.reshape(1).astype(jnp.int32)
    packed, mine = call(
        pack_kernel,
        in_vmem(7),
        [((4, ROWS, 128), BF16, True), ((128, 128), BF16, INTERPRET)],
        (0, 1500000),
        out_specs=(pl.BlockSpec(memory_space=pl.ANY), *in_vmem(1)),
        scratch_shapes=[pltpu.VMEM((4, ROWS, 128), BF16), pltpu.SemaphoreType.DMA((4,))],
    )(
        mamba_input,
        gate_input,
        in_b,
        in_c,
        step_size,
        jnp.swapaxes(ssm_state, 2, 3),
        queries,
    )
    arrived = lax.all_to_all(packed, "tok", split_axis=0, concat_axis=0, tiled=True)
    arrived = held(arrived)
    before = lax.ppermute(mine, "tok", [(i, (i + 1) % 4) for i in range(4)])
    rate = jnp.pad(lax.dynamic_slice(decay_rate, (tok * 4,), (4,)), (0, 124)).reshape(1, 128)
    skip = jnp.repeat(lax.dynamic_slice(skip_weight, (tok * 4,), (4,)), 64).reshape(1, 256)
    gain = lax.dynamic_slice(norm_gain, (tok * 256,), (256,)).reshape(1, 256)
    shares, run, pair = call(
        mixer_kernel,
        in_vmem(1) + [pl.BlockSpec(memory_space=pl.ANY)] + in_vmem(5),
        [
            ((32, 8, WIDTH), BF16, True),
            ((128, 128), F32, INTERPRET),
            ((2, 128, 128), BF16, INTERPRET),
        ],
        (400000000, 4000000),
        out_specs=(pl.BlockSpec(memory_space=pl.ANY), *in_vmem(2)),
        scratch_shapes=[
            pltpu.VMEM((256, 4096), BF16),
            pltpu.VMEM((32, 8, WIDTH), BF16),
            pltpu.SemaphoreType.DMA,
            pltpu.SemaphoreType.DMA((5,)),
        ],
    )(arrived, out_weight, held(rate), held(skip), held(gain), held(mine), held(before))
    farther = lax.ppermute(pair, "tok", [(i, (i + 2) % 4) for i in range(4)])
    landed = lax.all_to_all(shares, ("head", "tok"), split_axis=0, concat_axis=0, tiled=True)
    cached = (cached_key_rows, cache_values, draft_token_keys, draft_values)
    back = ((BACK_ROWS, 128), BF16, INTERPRET)
    near, last, states = call(
        near_kernel,
        in_smem(3) + in_vmem(8),
        [back, back, ((2, 128, 128), BF16, INTERPRET)],
        (0, 0),
        scratch_shapes=[pltpu.VMEM((4, 128, 128), BF16)],
    )(where, cache_len, accepted, arrived, held(pair), held(run), held(rate), *cached)
    after, across = call(far_kernel, in_smem(2) + in_vmem(6), [back, back], (0, 0))(
        where, cache_len, held(farther), held(states), *cached
    )
    returned = [held(near)] + [
        held(lax.ppermute(part, "tok", [(i, (i + shift) % 4) for i in range(4)]))
        for shift, part in ((1, after), (2, across), (3, last))
    ]
    attn_context, state_t = call(
        combine_kernel,
        in_smem(1) + in_vmem(4),
        [((2, 16, 512), BF16, True), ((2, 16, 32, 64), BF16, True)],
        (0, 0),
    )(where, *returned)
    (mamba_out,) = call(
        sum_kernel, in_vmem(1), [((2, 2, 4096), BF16, True)], (1000000, 1500000)
    )(held(landed))
    return (mamba_out, attn_context, jnp.swapaxes(state_t, 2, 3))


def solution(mesh):
    in_specs = (
        P("dp", "tok", "head"),
        P("dp", "tok", "head"),
        P("dp", "tok", "head"),
        P("dp", "tok", "head"),
        P("dp", "tok", "head"),
        P("head"),
        P("head"),
        P("head"),
        P("dp", "head", None, "tok"),
        P(("head", "tok"), None),
        P("dp", "tok", "head"),
        P("dp", "tok", "head"),
        P("dp", "tok", "head"),
        P("dp", "tok", "head"),
        P("dp", "tok", "head"),
        P("dp"),
        P("dp"),
    )
    out_specs = (
        P(("head", "tok"), "dp", None),
        P("dp", "tok", "head"),
        P("dp", "head", None, "tok"),
    )
    return jax.shard_map(body, mesh=mesh, in_specs=in_specs, out_specs=out_specs, check_vma=False)
```
